256 devices in a mesh: val: 8 (over x_lo, y), col: 32 (over x_hi, z, core).
Axes of the slice: x: 4 (x_hi: 2, x_lo: 2; x = x_hi * 2 + x_lo), y: 4, z: 8, core: 2. Of those that a mesh axis runs over, the one named last changes fastest.
Arguments:
- valence_store: float32 [8, 32, 2, 48, 2304], P('val', 'col'), may hold values from -6 to 6
- band_owner: int32 [8], replicated, may hold values from 0 to 31
- valence_energy: float32 [8], P('val'), may hold values from -8 to -1
- cond_bands: float32 [128, 2, 48, 2304], P('col'), may hold values from -6 to 6
- cond_energy: float32 [128], P('col'), may hold values from 0.5 to 10
- gvec_index: int32 [4096], replicated, may hold values from 0 to 110591, as said below
Outputs:
- chi_zero: float32 [2, 512, 4096], P(None, 'val', 'col')
The draws below stay inside these ranges and needn't reach their ends.
Inputs may be any that keep to these rules, and one draw needn't show every extreme that they name: `gvec_index`: distinct grid indices; entry 0 is 0 (the zero vector) and entry 1 is 110591.
All inputs are finite; a program needn't handle non-finite values.
Results may differ from the reference program's by a relative error of at most 0.0038.
Values may be sent and summed in bfloat16 or wider, within the bound.
No kernel may reach another device: no remote copies, remote signals or barrier semaphores. Data moves between devices by JAX's collectives and lax.ppermute only.
A program may use at most 256 MiB of HBM per device.

```python
import jax
import jax.numpy as jnp
from jax import lax

L = 48
NG = 4096
C_DEV = 4
ROW_DEV = 64
VB = 8
CB = 128
N_VAL = 8
N_COL = 32


def draw_gvec_index(key, part):
    others = 1 + jax.random.permutation(key, L * L * L - 2)[:NG - 2]
    fixed_ends = jnp.array([0, L * L * L - 1], dtype=jnp.int32)
    return jnp.concatenate([fixed_ends, others.astype(jnp.int32)])


def touch_ends(entries, stream_key, smallest, largest):
    dims = entries.shape
    index_at = [jax.random.randint(jax.random.fold_in(stream_key, axis), (), 0, dims[axis]) for axis in range(len(dims))]
    entries = entries.at[tuple(index_at)].set(smallest)
    longest = dims.index(max(dims))
    index_at[longest] = (index_at[longest] + 1) % dims[longest]
    return entries.at[tuple(index_at)].set(largest)


def level_of(key, extent, shards, low, top_value):
    gain = 1.0
    for position, blocks in shards:
        steps = jax.random.uniform(jax.random.fold_in(jax.random.fold_in(key, 6), position), (blocks,), jnp.float32, low / len(shards), top_value / len(shards))
        gain = gain * jnp.repeat(jnp.exp(steps), extent[position] // blocks).reshape((-1,) + (1,) * (len(extent) - 1 - position))
    return gain


def gaussian(own_key, dims, deviation, most, shards=(), kind=jnp.bfloat16):
    gain = level_of(own_key, dims, shards, -0.22, 0.18) if shards else 1.0
    result = jax.random.normal(own_key, dims, jnp.float32) * deviation * gain
    return jnp.minimum(jnp.maximum(result, -most), most).astype(kind)


def setup_inputs(seed: int = 0) -> dict:
    key_of = jax.random.split(jax.random.key(seed), 7)
    return {
        "valence_store": gaussian(key_of[0], (VB, N_COL, 2, L, L * L), 1.0, 6.0, ((0, 8), (1, 32)), jnp.float32),
        "band_owner": touch_ends(jax.random.randint(key_of[1], (VB,), 0, N_COL), jax.random.fold_in(key_of[1], 1), 0, N_COL - 1).astype(jnp.int32),
        "valence_energy": jnp.clip(-8.0 + 7.0 * jax.random.uniform(key_of[2], (VB,), jnp.float32) ** level_of(key_of[2], (VB,), ((0, 8),), -0.2, 0.2), -8.0, -1.0),
        "cond_bands": gaussian(key_of[3], (CB, 2, L, L * L), 1.0, 6.0, ((0, 32),), jnp.float32),
        "cond_energy": jnp.clip(0.5 + 9.5 * jax.random.uniform(key_of[4], (CB,), jnp.float32) ** level_of(key_of[4], (CB,), ((0, 32),), -0.2, 0.2), 0.5, 10.0),
        "gvec_index": draw_gvec_index(jax.random.fold_in(key_of[6], 71), 0),
    }


def pair_block(valence, cond_block, scaling, gvec_index):
    grid_side = cond_block.shape[2]
    real_part = valence[0] * cond_block[:, 0] + valence[1] * cond_block[:, 1]
    imag_part = valence[0] * cond_block[:, 1] - valence[1] * cond_block[:, 0]
    field = lax.complex(real_part, imag_part).reshape(-1, grid_side, grid_side, grid_side)
    spectrum = jnp.fft.fftn(field, axes=(1, 2, 3)).reshape(field.shape[0], -1)
    picked = jnp.take(spectrum, gvec_index, axis=1)
    scaled_real = scaling[:, None] * jnp.real(picked)
    scaled_imag = scaling[:, None] * jnp.imag(picked)
    return jnp.stack([scaled_real, scaled_imag], 1).astype(jnp.bfloat16)

def reference(valence_store, band_owner, valence_energy, cond_bands, cond_energy, gvec_index):
    val_count = valence_energy.shape[0]
    cond_count = cond_energy.shape[0]
    row_count = ROW_DEV * N_VAL
    constant = (cond_count * val_count) ** (-0.25) * L ** (-1.5)
    blocks = cond_bands.reshape(N_COL, C_DEV, 2, L, L * L)
    energy_blocks = cond_energy.reshape(N_COL, C_DEV)
    real_sum = jnp.zeros((row_count, NG), jnp.float32)
    imag_sum = jnp.zeros((row_count, NG), jnp.float32)
    for band_index in range(val_count):
        valence = valence_store[band_index, band_owner[band_index]]
        valence_level = valence_energy[band_index]

        def add_block(carried, inputs):
            cond_block, energies = inputs
            scaling = jnp.sqrt(2.0 / (energies - valence_level)) * constant
            pairs = pair_block(valence, cond_block, scaling, gvec_index)
            head_real = pairs[:, 0, :row_count]
            head_imag = pairs[:, 1, :row_count]
            real_new = carried[0] + jnp.dot(head_real.T, pairs[:, 0], preferred_element_type=jnp.float32) + jnp.dot(head_imag.T, pairs[:, 1], preferred_element_type=jnp.float32)
            imag_new = carried[1] + jnp.dot(head_imag.T, pairs[:, 0], preferred_element_type=jnp.float32) - jnp.dot(head_real.T, pairs[:, 1], preferred_element_type=jnp.float32)
            return ((real_new, imag_new), None)
        (real_sum, imag_sum), unused = lax.scan(add_block, (real_sum, imag_sum), (blocks, energy_blocks))
    return -jnp.stack([real_sum, imag_sum], 0)
```

```python
import numpy as np

import jax
import jax.numpy as jnp
from jax import lax
from jax.experimental import pallas as pl
from jax.experimental.pallas import tpu as pltpu
from jax.sharding import PartitionSpec as P

ROW_DEV = 64
L = 48
YI = 8
YB = L // YI
SLAB = YI * L
R1 = YB * L
K1 = 6 * R1
K1P = 1792
K2 = 6 * SLAB
BF = jnp.bfloat16
F32 = jnp.float32


def tables():
    def trig(phase):
        angle = 2.0 * np.pi * (phase % L) / L
        return np.stack([np.cos(angle), np.sin(angle)]).astype(np.float32)

    r = np.arange(L)
    x_of = np.tile(r, YB)
    yb_of = np.repeat(np.arange(YB), L)
    t1a = trig(r[:, None] * x_of[None, :])
    t1b = trig(8 * np.arange(8)[:, None] * yb_of[None, :])
    ka_of = np.repeat(np.arange(YI), L)
    kz_of = np.tile(r, YI)
    t2a = trig(r[:, None] * kz_of[None, :])
    t2b = trig(6 * np.arange(YI)[:, None] * ka_of[None, :])
    yi_of = np.repeat(np.arange(YI), L)
    tw = trig(np.arange(8)[:, None] * yi_of[None, :])
    return t1a, t1b, t2a, t2b, tw


def split(value):
    hi = value.astype(BF)
    return hi, (value - hi.astype(F32)).astype(BF)


def pairs_kernel(word, v_ref, c_ref, scale_ref, t1a, t1b, t2a, t2b, tw, out_ref, a1, b2, p3, z1, l2, y2, grid):
    step = pl.program_id(0)

    @pl.when(step == 0)
    def _():
        a1[:, K1:K1P] = jnp.zeros((2 * R1, K1P - K1), BF)
        p3[K1:K1P, :] = jnp.zeros((K1P - K1, 2 * SLAB), BF)
        for kb in range(YB):
            cb = t1b[0, kb:kb + 1, :]
            sb = t1b[1, kb:kb + 1, :]
            cos = t1a[0] * cb - t1a[1] * sb
            sin = t1a[1] * cb + t1a[0] * sb
            top = jnp.concatenate([cos, sin], 1)
            low = jnp.concatenate([-sin, cos], 1)
            for ri, value in enumerate((top, low)):
                hi, lo = split(value)
                r0 = ri * R1 + kb * L
                a1[r0:r0 + L, 0:2 * R1] = hi
                a1[r0:r0 + L, 2 * R1:4 * R1] = lo
                a1[r0:r0 + L, 4 * R1:6 * R1] = hi
        for yi in range(YI):
            cb = t2b[0, yi:yi + 1, :]
            sb = t2b[1, yi:yi + 1, :]
            cos = t2a[0] * cb - t2a[1] * sb
            sin = t2a[1] * cb + t2a[0] * sb
            for ri, value in enumerate((jnp.concatenate([cos, -sin], 1), jnp.concatenate([sin, cos], 1))):
                hi, lo = split(value)
                r0 = ri * SLAB + yi * L
                b2[r0:r0 + L, :] = hi
                b2[2 * SLAB + r0:2 * SLAB + r0 + L, :] = lo
                b2[4 * SLAB + r0:4 * SLAB + r0 + L, :] = hi

    for yb in range(YB):
        lanes = slice(yb * SLAB, (yb + 1) * SLAB)
        v0 = v_ref[0, :, lanes]
        v1 = v_ref[1, :, lanes]
        for bb in range(2):
            c0 = c_ref[bb, 0, :, lanes]
            c1 = c_ref[bb, 1, :, lanes]
            for ri, value in enumerate((v0 * c0 + v1 * c1, v0 * c1 - v1 * c0)):
                hi, lo = split(value)
                r0 = ri * R1 + yb * L
                cols = slice(bb * SLAB, (bb + 1) * SLAB)
                p3[r0:r0 + L, cols] = hi
                p3[2 * R1 + r0:2 * R1 + r0 + L, cols] = hi
                p3[4 * R1 + r0:4 * R1 + r0 + L, cols] = lo
    z1[...] = jnp.dot(a1[...], p3[...], preferred_element_type=F32)
    for kb in range(YB):
        cw = tw[0, kb:kb + 1, :]
        sw = tw[1, kb:kb + 1, :]
        for bb in range(2):
            cols = slice(bb * SLAB, (bb + 1) * SLAB)
            zr = z1[kb * L:kb * L + L, cols]
            zi = z1[R1 + kb * L:R1 + kb * L + L, cols]
            rows = slice(bb * R1 + kb * L, bb * R1 + kb * L + L)
            for ri, value in enumerate((zr * cw + zi * sw, zi * cw - zr * sw)):
                hi, lo = split(value)
                l2[rows, ri * SLAB:(ri + 1) * SLAB] = hi
                l2[rows, (2 + ri) * SLAB:(3 + ri) * SLAB] = hi
                l2[rows, (4 + ri) * SLAB:(5 + ri) * SLAB] = lo
    y2[...] = jnp.dot(l2[...], b2[...], preferred_element_type=F32)
    for bb in range(2):
        for ri in range(2):
            for t in range(3):
                c0 = ri * SLAB + t * 128
                start = t * 8 + ri * 4 + bb + 2 * step
                grid[pl.ds(start, R1, stride=24), :] = y2[bb * R1:(bb + 1) * R1, c0:c0 + 128]

    @pl.when(step == 1)
    def _():
        lane = lax.broadcasted_iota(jnp.int32, (8, 128), 1)
        scale = scale_ref[...]

        def block(p, carry):
            outs = []
            for h in range(2):
                accs = [jnp.zeros((8, 128), F32) for _ in range(4)]
                for i in range(128):
                    w = word[(2 * p + h) * 128 + i]
                    start = pl.multiple_of((w >> 7) * 8, 8)
                    row = pltpu.roll(grid[pl.ds(start, 8), :], w & 127, 1)
                    accs[i % 4] = jnp.where(lane == i, row, accs[i % 4])
                outs.append(((accs[0] + accs[1]) + (accs[2] + accs[3])) * scale)
            out_ref[pl.ds(pl.multiple_of(p * 16, 16), 16), :] = jnp.concatenate(outs, 0).astype(BF)
            return carry

        lax.fori_loop(0, out_ref.shape[0] // 16, block, 0)


def pair_elements(valence, cond, scale, words):
    count = words.shape[0]
    rows = count // 128 * 8
    full = lambda *shape: pl.BlockSpec(shape, lambda s, w: (0,) * len(shape))
    consts = tables()
    return pl.pallas_call(
        pairs_kernel,
        out_shape=jax.ShapeDtypeStruct((rows, 128), BF),
        grid_spec=pltpu.PrefetchScalarGridSpec(
            num_scalar_prefetch=1,
            grid=(2,),
            in_specs=[
                full(2, L, L * L),
                pl.BlockSpec((2, 2, L, L * L), lambda s, w: (s, 0, 0, 0)),
                full(8, 128),
            ] + [full(*c.shape) for c in consts],
            out_specs=full(rows, 128),
            scratch_shapes=[
                pltpu.VMEM((2 * R1, K1P), BF),
                pltpu.VMEM((K2, 2 * SLAB), BF),
                pltpu.VMEM((K1P, 2 * SLAB), BF),
                pltpu.VMEM((2 * R1, 2 * SLAB), F32),
                pltpu.VMEM((2 * R1, K2), BF),
                pltpu.VMEM((2 * R1, 2 * SLAB), F32),
                pltpu.VMEM((R1 * 24, 128), F32),
            ],
        ),
        compiler_params=pltpu.CompilerParams(
            dimension_semantics=("arbitrary",), vmem_limit_bytes=50 << 20
        ),
        name="pairs",
    )(words, valence, cond, scale, *[jnp.asarray(c) for c in consts])


def gather_words(gvec_index):
    kx = gvec_index // (L * L)
    ky = gvec_index // L % L
    kz = gvec_index % L
    lane = ky // YB * L + kz
    tile = (ky % YB * L + kx) * 3 + lane // 128
    place = lax.iota(jnp.int32, gvec_index.shape[0])
    return tile * 128 + (place - lane) % 128


def local(valence_store, band_owner, valence_energy, cond_bands, cond_energy, gvec_index):
    n_col = lax.axis_size("col")
    n_val = lax.axis_size("val")
    chips = n_col // 2
    me = lax.axis_index("col")
    core = me % 2
    owner = band_owner[lax.axis_index("val")]

    tiles = valence_store[0, 0].astype(jnp.float16).reshape(2, 6, 8, 18, 128)
    tiles = tiles.transpose(0, 1, 3, 2, 4).reshape(2, 108, 8, 128)
    tiles = jnp.pad(tiles, ((0, 0), (0, 4), (0, 0), (0, 0)))
    swap = [(i, i ^ 1) for i in range(n_col)]
    mine = lax.dynamic_index_in_dim(tiles, core, 0, False)
    theirs = lax.dynamic_index_in_dim(tiles, 1 - core, 0, False)
    other = lax.ppermute(theirs, "col", swap)
    half = jnp.where(owner % 2 == core, mine, other)
    groups = [[q * 2 + c for q in range(chips)] for c in range(2)]
    got = lax.all_to_all(half.reshape(chips, 7, 8, 128), "col", 0, 0, tiled=True, axis_index_groups=groups)
    chunk = lax.dynamic_index_in_dim(got, owner // 2, 0, True)
    again = jnp.broadcast_to(chunk, (chips, 7, 8, 128))
    half = lax.all_to_all(again, "col", 0, 0, tiled=True, axis_index_groups=groups).reshape(112, 8, 128)
    other = lax.ppermute(half, "col", swap)
    both = jnp.stack([jnp.where(core == 0, half, other), jnp.where(core == 0, other, half)], 0)
    valence = both[:, :108].reshape(2, 6, 18, 8, 128).transpose(0, 1, 3, 2, 4).reshape(2, L, L * L).astype(F32)

    total_bands = cond_bands.shape[0] * n_col * n_val
    constant = total_bands ** (-0.25) * L ** (-1.5)
    scaling = jnp.sqrt(2.0 / (cond_energy - valence_energy[0])) * constant
    scale = jnp.broadcast_to(jnp.concatenate([scaling, scaling])[:, None], (8, 128))
    pairs = pair_elements(valence, cond_bands, scale, gather_words(gvec_index)).reshape(n_col, 8, 128)

    row_count = ROW_DEV * n_val
    row_blocks = row_count // 128
    heads = jnp.broadcast_to(pairs[None, :row_blocks], (n_col, row_blocks, 8, 128))
    sent = jnp.concatenate([pairs[:, None], heads], 1)
    came = lax.all_to_all(sent, "col", 0, 0, tiled=True)
    col = came[:, 0]
    turned = jnp.concatenate([-col[:, 4:], col[:, :4]], 1)
    right = jnp.concatenate([col, turned], 2).reshape(n_col * 8, 256)
    left = came[:, 1:].transpose(1, 0, 2, 3).reshape(row_blocks, n_col * 8, 128)
    part = -lax.dot_general(
        left, right, (((1,), (0,)), ((), ())), preferred_element_type=F32
    )
    part = part.reshape(n_val, ROW_DEV, 256).astype(BF)
    summands = lax.all_to_all(part, "val", 0, 0, tiled=True)
    total = jnp.sum(summands.astype(F32), 0)
    return total.reshape(ROW_DEV, 2, 128).transpose(1, 0, 2)


def solution(mesh):
    return jax.shard_map(
        local,
        mesh=mesh,
        in_specs=(
            P("val", "col", None, None, None),
            P(),
            P("val"),
            P("col", None, None, None),
            P("col"),
            P(),
        ),
        out_specs=P(None, "val", "col"),
        check_vma=False,
    )
```

```python
import numpy as np

import jax
import jax.numpy as jnp
from jax import lax
from jax.experimental import pallas as pl
from jax.experimental.pallas import tpu as pltpu
from jax.sharding import PartitionSpec as P

ROW_DEV = 64
L = 48
YI = 8
YB = L // YI
SLAB = YI * L
R1 = YB * L
K1 = 6 * L
K2 = 6 * SLAB
ROOT = 0.75 ** 0.5
BF = jnp.bfloat16
F32 = jnp.float32


def tables():
    def trig(phase):
        angle = 2.0 * np.pi * (phase % L) / L
        return np.stack([np.cos(angle), np.sin(angle)]).astype(np.float32)

    r = np.arange(L)
    ka_of = np.repeat(np.arange(YI), L)
    kz_of = np.tile(r, YI)
    t1 = trig(r[:, None] * r[None, :])
    t1 = np.block([[t1[0], t1[1]], [-t1[1], t1[0]]])
    t2a = trig(r[:, None] * kz_of[None, :])
    t2b = trig(6 * np.arange(YI)[:, None] * ka_of[None, :])
    yi_of = np.repeat(np.arange(YI), L)
    tw = trig(np.arange(8)[:, None] * yi_of[None, :])
    return t1, t2a, t2b, tw


def split(value):
    hi = value.astype(BF)
    return hi, (value - hi.astype(F32)).astype(BF)


def dft3(s):
    (r0, i0), (r1, i1), (r2, i2) = s
    tr, ti = r1 + r2, i1 + i2
    ur, ui = r0 - 0.5 * tr, i0 - 0.5 * ti
    dr, di = (r1 - r2) * ROOT, (i1 - i2) * ROOT
    return [(r0 + tr, i0 + ti), (ur + di, ui - dr), (ur - di, ui + dr)]


def dft6(p):
    a = [(p[m][0] + p[m + 3][0], p[m][1] + p[m + 3][1]) for m in range(3)]
    b = [(p[m][0] - p[m + 3][0], p[m][1] - p[m + 3][1]) for m in range(3)]
    b[1] = (p[4][0] - p[1][0], p[4][1] - p[1][1])
    even = dft3(a)
    odd = dft3(b)
    return [even[0], odd[2], even[1], odd[0], even[2], odd[1]]


def pairs_kernel(word, v_ref, c_ref, scale_ref, t1, t2a, t2b, tw, out_ref, a1, b2, p3, l2, grid):
    step = pl.program_id(0)

    @pl.when(step == 0)
    def _():
        hi, lo = split(t1[...])
        a1[:, 0:2 * L] = hi
        a1[:, 2 * L:4 * L] = lo
        a1[:, 4 * L:6 * L] = hi
        for yi in range(YI):
            cb = t2b[0, yi:yi + 1, :]
            sb = t2b[1, yi:yi + 1, :]
            cos = t2a[0] * cb - t2a[1] * sb
            sin = t2a[1] * cb + t2a[0] * sb
            for value, negative, spots in ((cos, False, ((0, 0), (1, 1))), (sin, True, ((1, 0), (0, 1)))):
                hi, lo = split(value)
                for ri, half in spots:
                    flip = negative and ri == 0
                    high, low = (-hi, -lo) if flip else (hi, lo)
                    cols = slice(half * SLAB, (half + 1) * SLAB)
                    r0 = ri * SLAB + yi * L
                    b2[r0:r0 + L, cols] = high
                    b2[2 * SLAB + r0:2 * SLAB + r0 + L, cols] = low
                    b2[4 * SLAB + r0:4 * SLAB + r0 + L, cols] = high

    for lt in range(SLAB // 128):
        for xc in range(L // 16):
            xs = slice(xc * 16, xc * 16 + 16)
            for bb in range(2):
                cols = slice(bb * SLAB + lt * 128, bb * SLAB + lt * 128 + 128)
                p = []
                for yb in range(YB):
                    lanes = slice(yb * SLAB + lt * 128, yb * SLAB + lt * 128 + 128)
                    v0 = v_ref[0, xs, lanes]
                    v1 = v_ref[1, xs, lanes]
                    c0 = c_ref[bb, 0, xs, lanes]
                    c1 = c_ref[bb, 1, xs, lanes]
                    p.append((v0 * c0 + v1 * c1, v0 * c1 - v1 * c0))
                for kb, q in enumerate(dft6(p)):
                    for ri in range(2):
                        hi, lo = split(q[ri])
                        r0 = ri * L + xc * 16
                        p3[kb, r0:r0 + 16, cols] = hi
                        p3[kb, 2 * L + r0:2 * L + r0 + 16, cols] = hi
                        p3[kb, 4 * L + r0:4 * L + r0 + 16, cols] = lo
    for kb in range(YB):
        z = jnp.dot(a1[...], p3[kb], preferred_element_type=F32)
        cw = tw[0, kb:kb + 1, :]
        sw = tw[1, kb:kb + 1, :]
        for bb in range(2):
            zr = z[:L, bb * SLAB:(bb + 1) * SLAB]
            zi = z[L:, bb * SLAB:(bb + 1) * SLAB]
            rows = slice(bb * R1 + kb * L, bb * R1 + kb * L + L)
            for ri, value in enumerate((zr * cw + zi * sw, zi * cw - zr * sw)):
                hi, lo = split(value)
                l2[rows, ri * SLAB:(ri + 1) * SLAB] = hi
                l2[rows, (2 + ri) * SLAB:(3 + ri) * SLAB] = hi
                l2[rows, (4 + ri) * SLAB:(5 + ri) * SLAB] = lo
    y = jnp.dot(l2[...], b2[...], preferred_element_type=F32)
    for bb in range(2):
        for ri in range(2):
            for t in range(3):
                c0 = ri * SLAB + t * 128
                start = t * 8 + ri * 4 + bb + 2 * step
                grid[pl.ds(start, R1, stride=24), :] = y[bb * R1:(bb + 1) * R1, c0:c0 + 128]

    lane = lax.broadcasted_iota(jnp.int32, (8, 128), 1)

    def block(p):
        outs = []
        for h in range(2):
            accs = [jnp.zeros((8, 128), F32) for _ in range(4)]
            for i in range(128):
                w = word[(2 * p + h) * 128 + i]
                start = pl.multiple_of(w >> 7, 8)
                row = pltpu.roll(grid[pl.ds(start, 8), :], w & 127, 1)
                accs[i % 4] = jnp.where(lane == i, row, accs[i % 4])
            outs.append(((accs[0] + accs[1]) + (accs[2] + accs[3])) * scale_ref[...])
        out_ref[p * 16:p * 16 + 16, :] = jnp.concatenate(outs, 0).astype(BF)

    for p in range(out_ref.shape[0] // 16):
        pl.when(step == 1)(lambda p=p: block(p))


def pair_elements(valence, cond, scale, words):
    count = words.shape[0]
    rows = count // 128 * 8
    full = lambda *shape: pl.BlockSpec(shape, lambda s, w: (0,) * len(shape))
    consts = tables()
    return pl.pallas_call(
        pairs_kernel,
        out_shape=jax.ShapeDtypeStruct((rows, 128), BF),
        grid_spec=pltpu.PrefetchScalarGridSpec(
            num_scalar_prefetch=1,
            grid=(2,),
            in_specs=[
                full(2, L, L * L),
                pl.BlockSpec((2, 2, L, L * L), lambda s, w: (s, 0, 0, 0)),
                full(8, 128),
            ] + [full(*c.shape) for c in consts],
            out_specs=full(rows, 128),
            scratch_shapes=[
                pltpu.VMEM((2 * L, K1), BF),
                pltpu.VMEM((K2, 2 * SLAB), BF),
                pltpu.VMEM((YB, K1, 2 * SLAB), BF),
                pltpu.VMEM((2 * R1, K2), BF),
                pltpu.VMEM((R1 * 24, 128), F32),
            ],
        ),
        compiler_params=pltpu.CompilerParams(
            dimension_semantics=("arbitrary",), vmem_limit_bytes=50 << 20
        ),
        name="pairs",
    )(words, valence, cond, scale, *[jnp.asarray(c) for c in consts])


def gather_words(gvec_index):
    kx = gvec_index // (L * L)
    ky = gvec_index // L % L
    kz = gvec_index % L
    lane = ky // YB * L + kz
    tile = (ky % YB * L + kx) * 3 + lane // 128
    place = lax.iota(jnp.int32, gvec_index.shape[0])
    return tile * 1024 + (place - lane) % 128


def local(valence_store, band_owner, valence_energy, cond_bands, cond_energy, gvec_index):
    n_col = lax.axis_size("col")
    n_val = lax.axis_size("val")
    chips = n_col // 2
    me = lax.axis_index("col")
    core = me % 2
    owner = band_owner[lax.axis_index("val")]

    tiles = valence_store[0, 0].astype(jnp.float16).reshape(2, 6, 8, 18, 128)
    tiles = tiles.transpose(0, 1, 3, 2, 4).reshape(2, 108, 8, 128)
    tiles = jnp.pad(tiles, ((0, 0), (0, 4), (0, 0), (0, 0)))
    swap = [(i, i ^ 1) for i in range(n_col)]
    mine = lax.dynamic_index_in_dim(tiles, core, 0, False)
    theirs = lax.dynamic_index_in_dim(tiles, 1 - core, 0, False)
    other = lax.ppermute(theirs, "col", swap)
    half = jnp.where(owner % 2 == core, mine, other)
    groups = [[q * 2 + c for q in range(chips)] for c in range(2)]
    got = lax.all_to_all(half.reshape(chips, 7, 8, 128), "col", 0, 0, tiled=True, axis_index_groups=groups)
    chunk = lax.dynamic_index_in_dim(got, owner // 2, 0, True)
    again = jnp.broadcast_to(chunk, (chips, 7, 8, 128))
    half = lax.all_to_all(again, "col", 0, 0, tiled=True, axis_index_groups=groups).reshape(112, 8, 128)
    other = lax.ppermute(half, "col", swap)
    both = jnp.stack([jnp.where(core == 0, half, other), jnp.where(core == 0, other, half)], 0)
    valence = both[:, :108].reshape(2, 6, 18, 8, 128).transpose(0, 1, 3, 2, 4).reshape(2, L, L * L).astype(F32)

    total_bands = cond_bands.shape[0] * n_col * n_val
    constant = total_bands ** (-0.25) * L ** (-1.5)
    scaling = jnp.sqrt(2.0 / (cond_energy - valence_energy[0])) * constant
    scale = jnp.broadcast_to(jnp.concatenate([scaling, scaling])[:, None], (8, 128))
    pairs = pair_elements(valence, cond_bands, scale, gather_words(gvec_index)).reshape(n_col, 8, 128)

    row_count = ROW_DEV * n_val
    row_blocks = row_count // 128
    heads = jnp.broadcast_to(pairs[None, :row_blocks], (n_col, row_blocks, 8, 128))
    sent = jnp.concatenate([pairs[:, None], heads], 1)
    came = lax.all_to_all(sent, "col", 0, 0, tiled=True)
    col = came[:, 0]
    turned = jnp.concatenate([-col[:, 4:], col[:, :4]], 1)
    right = jnp.concatenate([col, turned], 2).reshape(n_col * 8, 256)
    left = came[:, 1:].transpose(1, 0, 2, 3).reshape(row_blocks, n_col * 8, 128)
    part = -lax.dot_general(
        left, right, (((1,), (0,)), ((), ())), preferred_element_type=F32
    )
    part = part.reshape(n_val, ROW_DEV, 256).astype(BF)
    summands = lax.all_to_all(part, "val", 0, 0, tiled=True)
    total = jnp.sum(summands.astype(F32), 0)
    return total.reshape(ROW_DEV, 2, 128).transpose(1, 0, 2)


def solution(mesh):
    return jax.shard_map(
        local,
        mesh=mesh,
        in_specs=(
            P("val", "col", None, None, None),
            P(),
            P("val"),
            P("col", None, None, None),
            P("col"),
            P(),
        ),
        out_specs=P(None, "val", "col"),
        check_vma=False,
    )
```

```python
import numpy as np

import jax
import jax.numpy as jnp
from jax import lax
from jax.experimental import pallas as pl
from jax.experimental.pallas import tpu as pltpu
from jax.sharding import PartitionSpec as P

ROW_DEV = 64
L = 48
YI = 8
YB = L // YI
SLAB = YI * L
R1 = YB * L
K1 = 6 * L
K2 = 6 * SLAB
ROOT = 0.75 ** 0.5
BF = jnp.bfloat16
F32 = jnp.float32


def tables():
    def trig(phase):
        angle = 2.0 * np.pi * (phase % L) / L
        return np.stack([np.cos(angle), np.sin(angle)]).astype(np.float32)

    r = np.arange(L)
    ka_of = np.repeat(np.arange(YI), L)
    kz_of = np.tile(r, YI)
    t1 = trig(r[:, None] * r[None, :])
    t1 = np.block([[t1[0], t1[1]], [-t1[1], t1[0]]])
    t2a = trig(r[:, None] * kz_of[None, :])
    t2b = trig(6 * np.arange(YI)[:, None] * ka_of[None, :])
    yi_of = np.repeat(np.arange(YI), L)
    tw = trig(np.arange(8)[:, None] * yi_of[None, :])
    return t1, t2a, t2b, tw


def split(value):
    hi = value.astype(BF)
    return hi, (value - hi.astype(F32)).astype(BF)


def dft3(s):
    (r0, i0), (r1, i1), (r2, i2) = s
    tr, ti = r1 + r2, i1 + i2
    ur, ui = r0 - 0.5 * tr, i0 - 0.5 * ti
    dr, di = (r1 - r2) * ROOT, (i1 - i2) * ROOT
    return [(r0 + tr, i0 + ti), (ur + di, ui - dr), (ur - di, ui + dr)]


def dft6(p):
    a = [(p[m][0] + p[m + 3][0], p[m][1] + p[m + 3][1]) for m in range(3)]
    b = [(p[m][0] - p[m + 3][0], p[m][1] - p[m + 3][1]) for m in range(3)]
    b[1] = (p[4][0] - p[1][0], p[4][1] - p[1][1])
    even = dft3(a)
    odd = dft3(b)
    return [even[0], odd[2], even[1], odd[0], even[2], odd[1]]


def fill_tables(t1, t2a, t2b, a1, b2):
    hi, lo = split(t1[...])
    a1[:, 0:2 * L] = hi
    a1[:, 2 * L:4 * L] = lo
    a1[:, 4 * L:6 * L] = hi
    for yi in range(YI):
        cb = t2b[0, yi:yi + 1, :]
        sb = t2b[1, yi:yi + 1, :]
        cos = t2a[0] * cb - t2a[1] * sb
        sin = t2a[1] * cb + t2a[0] * sb
        for value, negative, spots in ((cos, False, ((0, 0), (1, 1))), (sin, True, ((1, 0), (0, 1)))):
            hi, lo = split(value)
            for ri, half in spots:
                flip = negative and ri == 0
                high, low = (-hi, -lo) if flip else (hi, lo)
                cols = slice(half * SLAB, (half + 1) * SLAB)
                r0 = ri * SLAB + yi * L
                b2[r0:r0 + L, cols] = high
                b2[2 * SLAB + r0:2 * SLAB + r0 + L, cols] = low
                b2[4 * SLAB + r0:4 * SLAB + r0 + L, cols] = high


def pairs_kernel(
    word_any, c_any, v_ref, scale_ref, t1, t2a, t2b, tw, hot_ref, out_ref,
    word, c_ref, a1, b2, p3, l2, grid, d0, d1, d2, d3, sems, word_sem,
):
    def fetch(step):
        pair = pl.ds(2 * step, 2)
        return pltpu.make_async_copy(c_any.at[pair], c_ref.at[pair], sems.at[step])

    word_copy = pltpu.make_async_copy(word_any, word, word_sem)
    fetch(0).start()
    fetch(1).start()
    word_copy.start()
    fill_tables(t1, t2a, t2b, a1, b2)

    def bands(step, carry):
        fetch(step).wait()
        for lt in range(SLAB // 128):
            for xc in range(L // 16):
                xs = slice(xc * 16, xc * 16 + 16)
                for bb in range(2):
                    cols = slice(bb * SLAB + lt * 128, bb * SLAB + lt * 128 + 128)
                    p = []
                    for yb in range(YB):
                        lanes = slice(yb * SLAB + lt * 128, yb * SLAB + lt * 128 + 128)
                        v0 = v_ref[0, xs, lanes]
                        v1 = v_ref[1, xs, lanes]
                        c0 = c_ref[2 * step + bb, 0, xs, lanes]
                        c1 = c_ref[2 * step + bb, 1, xs, lanes]
                        p.append((v0 * c0 + v1 * c1, v0 * c1 - v1 * c0))
                    for kb, q in enumerate(dft6(p)):
                        for ri in range(2):
                            hi, lo = split(q[ri])
                            r0 = ri * L + xc * 16
                            p3[kb, r0:r0 + 16, cols] = hi
                            p3[kb, 2 * L + r0:2 * L + r0 + 16, cols] = hi
                            p3[kb, 4 * L + r0:4 * L + r0 + 16, cols] = lo
        for kb in range(YB):
            z = jnp.dot(a1[...], p3[kb], preferred_element_type=F32)
            cw = tw[0, kb:kb + 1, :]
            sw = tw[1, kb:kb + 1, :]
            for bb in range(2):
                zr = z[:L, bb * SLAB:(bb + 1) * SLAB]
                zi = z[L:, bb * SLAB:(bb + 1) * SLAB]
                rows = slice(bb * R1 + kb * L, bb * R1 + kb * L + L)
                for ri, value in enumerate((zr * cw + zi * sw, zi * cw - zr * sw)):
                    hi, lo = split(value)
                    l2[rows, ri * SLAB:(ri + 1) * SLAB] = hi
                    l2[rows, (2 + ri) * SLAB:(3 + ri) * SLAB] = hi
                    l2[rows, (4 + ri) * SLAB:(5 + ri) * SLAB] = lo
        y = jnp.dot(l2[...], b2[...], preferred_element_type=F32)
        for bb in range(2):
            scale = scale_ref[pl.ds(2 * step + bb, 1), :]
            for ri in range(2):
                for t in range(3):
                    c0 = ri * SLAB + t * 128
                    start = t * 8 + ri * 4 + bb + 2 * step
                    grid[pl.ds(start, R1, stride=24), :] = y[bb * R1:(bb + 1) * R1, c0:c0 + 128] * scale
        return carry

    lax.fori_loop(0, 2, bands, 0)

    row = lax.broadcasted_iota(jnp.int32, (16, 8 * 128), 0)
    comp = lax.broadcasted_iota(jnp.int32, (16, 8 * 128), 1) // 128
    pick = [(row == comp + 8 * h).astype(F32).astype(BF) for h in range(2)]

    def copy(p, d, first, last):
        for j in range(first, last):
            h, i = divmod(j, 128)
            start = pl.multiple_of(word[p * 256 + j], 8)
            d[h][pl.ds(i // 8 * 64 + i % 8, 8, stride=8), :] = grid[pl.ds(start, 8), :]

    def partial_sum(p, d, k):
        h, c0 = divmod(2 * k, 8)
        hot = hot_ref[p * 256 + h * 128:p * 256 + h * 128 + 128, :]
        rows = []
        for c in (c0, c0 + 1):
            cell = jnp.concatenate([d[h][ib * 64 + c * 8:ib * 64 + c * 8 + 8, :] for ib in range(16)], 0)
            rows.append(cell.astype(BF) * hot)
        return lax.dot_general(
            pick[h][:, c0 * 128:c0 * 128 + 256], jnp.concatenate(rows, 1),
            (((1,), (1,)), ((), ())), preferred_element_type=F32,
        )

    word_copy.wait()
    buffers = (d0, d1), (d2, d3)
    count = out_ref.shape[0] // 16
    copy(0, buffers[0], 0, 256)
    for p in range(count):
        total = None
        for k in range(8):
            got = partial_sum(p, buffers[p % 2], k)
            total = got if total is None else total + got
            if p + 1 < count:
                copy(p + 1, buffers[(p + 1) % 2], 32 * k, 32 * k + 32)
        out_ref[p * 16:p * 16 + 16, :] = total.astype(BF)


def pair_elements(valence, cond, scale, words, hot):
    count = words.shape[0]
    rows = count // 128 * 8
    t1, t2a, t2b, tw = tables()
    vmem = pl.BlockSpec(memory_space=pltpu.VMEM)
    hbm = pl.BlockSpec(memory_space=pl.ANY)
    return pl.pallas_call(
        pairs_kernel,
        out_shape=jax.ShapeDtypeStruct((rows, 128), BF),
        in_specs=[hbm, hbm] + [vmem] * 7,
        out_specs=vmem,
        scratch_shapes=[
            pltpu.SMEM((count,), jnp.int32),
            pltpu.VMEM(cond.shape, F32),
            pltpu.VMEM((2 * L, K1), BF),
            pltpu.VMEM((K2, 2 * SLAB), BF),
            pltpu.VMEM((YB, K1, 2 * SLAB), BF),
            pltpu.VMEM((2 * R1, K2), BF),
            pltpu.VMEM((R1 * 24, 128), F32),
        ] + [pltpu.VMEM((8 * 128, 128), F32)] * 4 + [
            pltpu.SemaphoreType.DMA((2,)),
            pltpu.SemaphoreType.DMA(()),
        ],
        compiler_params=pltpu.CompilerParams(vmem_limit_bytes=40 << 20),
        name="pairs",
    )(words, cond, valence, scale, t1, t2a, t2b, tw, hot)


def gather_words(gvec_index):
    kx = gvec_index // (L * L)
    ky = gvec_index // L % L
    kz = gvec_index % L
    lane = ky // YB * L + kz
    tile = (ky % YB * L + kx) * 3 + lane // 128
    hot = (lane % 128)[:, None] == lax.iota(jnp.int32, 128)[None, :]
    return tile * 8, hot.astype(F32).astype(BF)


def local(valence_store, band_owner, valence_energy, cond_bands, cond_energy, gvec_index):
    n_col = lax.axis_size("col")
    n_val = lax.axis_size("val")
    chips = n_col // 2
    core = lax.axis_index("col") & 1
    bands = lax.iota(jnp.int32, band_owner.shape[0])
    owner = jnp.sum(jnp.where(bands == lax.axis_index("val"), band_owner, 0))
    spread = jnp.broadcast_to(band_owner[:, None], (band_owner.shape[0], 128))
    owner_core = jnp.sum(jnp.where(bands[:, None] == lax.axis_index("val"), spread, 0), 0) & 1

    tiles = valence_store[0, 0].astype(jnp.float16).reshape(2, 6, 8, 18, 128)
    tiles = tiles.transpose(0, 1, 3, 2, 4).reshape(2, 108, 8, 128)
    tiles = jnp.pad(tiles, ((0, 0), (0, 4), (0, 0), (0, 0)))
    swap = [(i, i ^ 1) for i in range(n_col)]
    mine = lax.dynamic_index_in_dim(tiles, core, 0, False)
    theirs = lax.dynamic_index_in_dim(tiles, 1 - core, 0, False)
    other = lax.ppermute(theirs, "col", swap)
    half = jnp.where(owner_core[None, None, :] == core, mine, other)
    groups = [[q * 2 + c for q in range(chips)] for c in range(2)]
    got = lax.all_to_all(half.reshape(chips, 7, 8, 128), "col", 0, 0, tiled=True, axis_index_groups=groups)
    chunk = lax.dynamic_index_in_dim(got, owner >> 1, 0, True)
    again = jnp.broadcast_to(chunk, (chips, 7, 8, 128))
    half = lax.all_to_all(again, "col", 0, 0, tiled=True, axis_index_groups=groups).reshape(112, 8, 128)
    other = lax.ppermute(half, "col", swap)
    both = jnp.stack([jnp.where(core == 0, half, other), jnp.where(core == 0, other, half)], 0)
    valence = both[:, :108].reshape(2, 6, 18, 8, 128).transpose(0, 1, 3, 2, 4).reshape(2, L, L * L).astype(F32)

    total_bands = cond_bands.shape[0] * n_col * n_val
    constant = total_bands ** (-0.25) * L ** (-1.5)
    scaling = jnp.sqrt(2.0 / (cond_energy - valence_energy[0])) * constant
    scale = jnp.broadcast_to(scaling[:, None], (scaling.shape[0], 128))
    pairs = pair_elements(valence, cond_bands, scale, *gather_words(gvec_index)).reshape(n_col, 8, 128)

    row_count = ROW_DEV * n_val
    row_blocks = row_count // 128
    heads = pairs[:row_blocks]
    by_core = pairs.reshape(chips, 2, 8, 128)
    mine = lax.dynamic_index_in_dim(by_core, core, 1, False)
    theirs = lax.dynamic_index_in_dim(by_core, 1 - core, 1, False)
    other = lax.ppermute(jnp.concatenate([theirs, heads], 0), "col", swap)
    spread = lambda block: jnp.broadcast_to(block[None], (chips, row_blocks, 8, 128))
    sent = jnp.concatenate(
        [mine[:, None], spread(heads), other[:chips, None], spread(other[chips:])], 1
    )
    came = lax.all_to_all(sent, "col", 0, 0, tiled=True, axis_index_groups=groups)
    came = came.reshape(n_col, 1 + row_blocks, 8, 128)
    col = came[:, 0]
    turned = jnp.concatenate([-col[:, 4:], col[:, :4]], 1)
    right = jnp.concatenate([col, turned], 2).reshape(n_col * 8, 256)
    left = came[:, 1:].transpose(1, 0, 2, 3).reshape(row_blocks, n_col * 8, 128)
    part = -lax.dot_general(
        left, right, (((1,), (0,)), ((), ())), preferred_element_type=F32
    )
    part = part.reshape(n_val, ROW_DEV, 256).astype(BF)
    summands = lax.all_to_all(part, "val", 0, 0, tiled=True)
    total = jnp.sum(summands.astype(F32), 0)
    return total.reshape(ROW_DEV, 2, 128).transpose(1, 0, 2)


def solution(mesh):
    return jax.shard_map(
        local,
        mesh=mesh,
        in_specs=(
            P("val", "col", None, None, None),
            P(),
            P("val"),
            P("col", None, None, None),
            P("col"),
            P(),
        ),
        out_specs=P(None, "val", "col"),
        check_vma=False,
    )
```

```python
import numpy as np

import jax
import jax.numpy as jnp
from jax import lax
from jax.experimental import pallas as pl
from jax.experimental.pallas import tpu as pltpu
from jax.sharding import PartitionSpec as P

ROW_DEV = 64
L = 48
YI = 8
YB = L // YI
SLAB = YI * L
R1 = YB * L
K1 = 6 * L
K2 = 6 * SLAB
ROOT = 0.75 ** 0.5
BF = jnp.bfloat16
F32 = jnp.float32


def tables():
    def trig(phase):
        angle = 2.0 * np.pi * (phase % L) / L
        return np.stack([np.cos(angle), np.sin(angle)]).astype(np.float32)

    r = np.arange(L)
    ka_of = np.repeat(np.arange(YI), L)
    kz_of = np.tile(r, YI)
    t1 = trig(r[:, None] * r[None, :])
    t1 = np.block([[t1[0], t1[1]], [-t1[1], t1[0]]])
    t2a = trig(r[:, None] * kz_of[None, :])
    t2b = trig(6 * np.arange(YI)[:, None] * ka_of[None, :])
    yi_of = np.repeat(np.arange(YI), L)
    tw = trig(np.arange(8)[:, None] * yi_of[None, :])
    return t1, t2a, t2b, tw


def split(value):
    hi = value.astype(BF)
    return hi, (value - hi.astype(F32)).astype(BF)


def dft3(s):
    (r0, i0), (r1, i1), (r2, i2) = s
    tr, ti = r1 + r2, i1 + i2
    ur, ui = r0 - 0.5 * tr, i0 - 0.5 * ti
    dr, di = (r1 - r2) * ROOT, (i1 - i2) * ROOT
    return [(r0 + tr, i0 + ti), (ur + di, ui - dr), (ur - di, ui + dr)]


def dft6(p):
    a = [(p[m][0] + p[m + 3][0], p[m][1] + p[m + 3][1]) for m in range(3)]
    b = [(p[m][0] - p[m + 3][0], p[m][1] - p[m + 3][1]) for m in range(3)]
    b[1] = (p[4][0] - p[1][0], p[4][1] - p[1][1])
    even = dft3(a)
    odd = dft3(b)
    return [even[0], odd[2], even[1], odd[0], even[2], odd[1]]


def table_kernel(t1, t2a, t2b, a1, b2):
    hi, lo = split(t1[...])
    a1[:, 0:2 * L] = hi
    a1[:, 2 * L:4 * L] = lo
    a1[:, 4 * L:6 * L] = hi
    for yi in range(YI):
        cb = t2b[0, yi:yi + 1, :]
        sb = t2b[1, yi:yi + 1, :]
        cos = t2a[0] * cb - t2a[1] * sb
        sin = t2a[1] * cb + t2a[0] * sb
        for value, negative, spots in ((cos, False, ((0, 0), (1, 1))), (sin, True, ((1, 0), (0, 1)))):
            hi, lo = split(value)
            for ri, half in spots:
                flip = negative and ri == 0
                high, low = (-hi, -lo) if flip else (hi, lo)
                cols = slice(half * SLAB, (half + 1) * SLAB)
                r0 = ri * SLAB + yi * L
                b2[r0:r0 + L, cols] = high
                b2[2 * SLAB + r0:2 * SLAB + r0 + L, cols] = low
                b2[4 * SLAB + r0:4 * SLAB + r0 + L, cols] = high


def pairs_kernel(
    word_any, c_any, b2_any, v_ref, scale_ref, tw, a1, hot_ref, out_ref,
    word, c_ref, b2, p3, l2, grid, d0, d1, d2, d3, sems, word_sem, b2_sem,
):
    def fetch(step):
        pair = pl.ds(2 * step, 2)
        return pltpu.make_async_copy(c_any.at[pair], c_ref.at[pair], sems.at[step])

    word_copy = pltpu.make_async_copy(word_any, word, word_sem)
    b2_copy = pltpu.make_async_copy(b2_any, b2, b2_sem)
    fetch(0).start()
    b2_copy.start()
    fetch(1).start()
    word_copy.start()

    def bands(step, carry):
        fetch(step).wait()
        for lt in range(SLAB // 128):
            for xc in range(L // 16):
                xs = slice(xc * 16, xc * 16 + 16)
                for bb in range(2):
                    cols = slice(bb * SLAB + lt * 128, bb * SLAB + lt * 128 + 128)
                    p = []
                    for yb in range(YB):
                        lanes = slice(yb * SLAB + lt * 128, yb * SLAB + lt * 128 + 128)
                        v0 = v_ref[0, xs, lanes]
                        v1 = v_ref[1, xs, lanes]
                        c0 = c_ref[2 * step + bb, 0, xs, lanes]
                        c1 = c_ref[2 * step + bb, 1, xs, lanes]
                        p.append((v0 * c0 + v1 * c1, v0 * c1 - v1 * c0))
                    for kb, q in enumerate(dft6(p)):
                        for ri in range(2):
                            hi, lo = split(q[ri])
                            r0 = ri * L + xc * 16
                            p3[kb, r0:r0 + 16, cols] = hi
                            p3[kb, 2 * L + r0:2 * L + r0 + 16, cols] = hi
                            p3[kb, 4 * L + r0:4 * L + r0 + 16, cols] = lo
        for kb in range(YB):
            z = jnp.dot(a1[...], p3[kb], preferred_element_type=F32)
            cw = tw[0, kb:kb + 1, :]
            sw = tw[1, kb:kb + 1, :]
            for bb in range(2):
                zr = z[:L, bb * SLAB:(bb + 1) * SLAB]
                zi = z[L:, bb * SLAB:(bb + 1) * SLAB]
                rows = slice(bb * R1 + kb * L, bb * R1 + kb * L + L)
                for ri, value in enumerate((zr * cw + zi * sw, zi * cw - zr * sw)):
                    hi, lo = split(value)
                    l2[rows, ri * SLAB:(ri + 1) * SLAB] = hi
                    l2[rows, (2 + ri) * SLAB:(3 + ri) * SLAB] = hi
                    l2[rows, (4 + ri) * SLAB:(5 + ri) * SLAB] = lo
        @pl.when(step == 0)
        def _():
            b2_copy.wait()

        y = jnp.dot(l2[...], b2[...], preferred_element_type=F32)
        for bb in range(2):
            scale = scale_ref[pl.ds(2 * step + bb, 1), :]
            for ri in range(2):
                for t in range(3):
                    c0 = ri * SLAB + t * 128
                    start = t * 8 + ri * 4 + bb + 2 * step
                    grid[pl.ds(start, R1, stride=24), :] = y[bb * R1:(bb + 1) * R1, c0:c0 + 128] * scale
        return carry

    lax.fori_loop(0, 2, bands, 0)

    row = lax.broadcasted_iota(jnp.int32, (16, 8 * 128), 0)
    comp = lax.broadcasted_iota(jnp.int32, (16, 8 * 128), 1) // 128
    pick = [(row == comp + 8 * h).astype(F32).astype(BF) for h in range(2)]

    def copy(p, d, first, last):
        for j in range(first, last):
            h, i = divmod(j, 128)
            start = pl.multiple_of(word[p * 256 + j], 8)
            d[h][pl.ds(i // 8 * 64 + i % 8, 8, stride=8), :] = grid[pl.ds(start, 8), :]

    def partial_sum(p, d, k):
        h, c0 = divmod(2 * k, 8)
        hot = hot_ref[p * 256 + h * 128:p * 256 + h * 128 + 128, :]
        rows = []
        for c in (c0, c0 + 1):
            cell = jnp.concatenate([d[h][ib * 64 + c * 8:ib * 64 + c * 8 + 8, :] for ib in range(16)], 0)
            rows.append(cell.astype(BF) * hot)
        return lax.dot_general(
            pick[h][:, c0 * 128:c0 * 128 + 256], jnp.concatenate(rows, 1),
            (((1,), (1,)), ((), ())), preferred_element_type=F32,
        )

    word_copy.wait()
    buffers = (d0, d1), (d2, d3)
    count = out_ref.shape[0] // 16
    copy(0, buffers[0], 0, 256)
    for p in range(count):
        total = None
        for k in range(8):
            got = partial_sum(p, buffers[p % 2], k)
            total = got if total is None else total + got
            if p + 1 < count:
                copy(p + 1, buffers[(p + 1) % 2], 32 * k, 32 * k + 32)
        out_ref[p * 16:p * 16 + 16, :] = total.astype(BF)


def dft_tables():
    t1, t2a, t2b, tw = tables()
    vmem = pl.BlockSpec(memory_space=pltpu.VMEM)
    a1, b2 = pl.pallas_call(
        table_kernel,
        out_shape=(
            jax.ShapeDtypeStruct((2 * L, K1), BF),
            jax.ShapeDtypeStruct((K2, 2 * SLAB), BF),
        ),
        in_specs=[vmem] * 3,
        out_specs=(vmem, vmem),
        name="dft_tables",
    )(t1, t2a, t2b)
    return a1, b2, jnp.asarray(tw)


def pair_elements(valence, cond, scale, words, hot, a1, b2, tw):
    count = words.shape[0]
    rows = count // 128 * 8
    vmem = pl.BlockSpec(memory_space=pltpu.VMEM)
    hbm = pl.BlockSpec(memory_space=pltpu.HBM)
    keep = lambda x: pltpu.with_memory_space_constraint(x, pltpu.HBM)
    return pl.pallas_call(
        pairs_kernel,
        out_shape=jax.ShapeDtypeStruct((rows, 128), BF),
        in_specs=[hbm, hbm, hbm] + [vmem] * 5,
        out_specs=vmem,
        scratch_shapes=[
            pltpu.SMEM((count,), jnp.int32),
            pltpu.VMEM(cond.shape, F32),
            pltpu.VMEM((K2, 2 * SLAB), BF),
            pltpu.VMEM((YB, K1, 2 * SLAB), BF),
            pltpu.VMEM((2 * R1, K2), BF),
            pltpu.VMEM((R1 * 24, 128), F32),
        ] + [pltpu.VMEM((8 * 128, 128), F32)] * 4 + [
            pltpu.SemaphoreType.DMA((2,)),
            pltpu.SemaphoreType.DMA(()),
            pltpu.SemaphoreType.DMA(()),
        ],
        compiler_params=pltpu.CompilerParams(vmem_limit_bytes=40 << 20),
        name="pairs",
    )(words, keep(cond), keep(b2), valence, scale, tw, a1, hot)


def gather_words(gvec_index):
    kx = gvec_index // (L * L)
    ky = gvec_index // L % L
    kz = gvec_index % L
    lane = ky // YB * L + kz
    tile = (ky % YB * L + kx) * 3 + lane // 128
    hot = (lane % 128)[:, None] == lax.iota(jnp.int32, 128)[None, :]
    return tile * 8, hot.astype(F32).astype(BF)


def local(valence_store, band_owner, valence_energy, cond_bands, cond_energy, gvec_index):
    n_col = lax.axis_size("col")
    n_val = lax.axis_size("val")
    chips = n_col // 2
    core = lax.axis_index("col") & 1
    bands = lax.iota(jnp.int32, band_owner.shape[0])
    owner = jnp.sum(jnp.where(bands == lax.axis_index("val"), band_owner, 0))
    spread = jnp.broadcast_to(band_owner[:, None], (band_owner.shape[0], 128))
    owner_core = jnp.sum(jnp.where(bands[:, None] == lax.axis_index("val"), spread, 0), 0) & 1

    tiles = valence_store[0, 0].astype(jnp.float16).reshape(2, 6, 8, 18, 128)
    tiles = tiles.transpose(0, 1, 3, 2, 4).reshape(2, 108, 8, 128)
    tiles = jnp.pad(tiles, ((0, 0), (0, 4), (0, 0), (0, 0)))
    swap = [(i, i ^ 1) for i in range(n_col)]
    mine = lax.dynamic_index_in_dim(tiles, core, 0, False)
    theirs = lax.dynamic_index_in_dim(tiles, 1 - core, 0, False)
    other = lax.ppermute(theirs, "col", swap)
    half = jnp.where(owner_core[None, None, :] == core, mine, other)
    groups = [[q * 2 + c for q in range(chips)] for c in range(2)]
    got = lax.all_to_all(half.reshape(chips, 7, 8, 128), "col", 0, 0, tiled=True, axis_index_groups=groups)
    total_bands = cond_bands.shape[0] * n_col * n_val
    constant = total_bands ** (-0.25) * L ** (-1.5)
    scaling = jnp.sqrt(2.0 / (cond_energy - valence_energy[0])) * constant
    scale = jnp.broadcast_to(scaling[:, None], (scaling.shape[0], 128))
    words, hot = gather_words(gvec_index)
    chunk = lax.dynamic_index_in_dim(got, owner >> 1, 0, True)
    chunk, scale, words, hot, tabs = lax.optimization_barrier((chunk, scale, words, hot, dft_tables()))
    again = jnp.broadcast_to(chunk, (chips, 7, 8, 128))
    half = lax.all_to_all(again, "col", 0, 0, tiled=True, axis_index_groups=groups).reshape(112, 8, 128)
    other = lax.ppermute(half, "col", swap)
    both = jnp.stack([jnp.where(core == 0, half, other), jnp.where(core == 0, other, half)], 0)
    valence = both[:, :108].reshape(2, 6, 18, 8, 128).transpose(0, 1, 3, 2, 4).reshape(2, L, L * L).astype(F32)

    pairs = pair_elements(valence, cond_bands, scale, words, hot, *tabs).reshape(n_col, 8, 128)

    row_count = ROW_DEV * n_val
    row_blocks = row_count // 128
    heads = pairs[:row_blocks]
    by_core = pairs.reshape(chips, 2, 8, 128)
    mine = lax.dynamic_index_in_dim(by_core, core, 1, False)
    theirs = lax.dynamic_index_in_dim(by_core, 1 - core, 1, False)
    other = lax.ppermute(jnp.concatenate([theirs, heads], 0), "col", swap)
    spread = lambda block: jnp.broadcast_to(block[None], (chips, row_blocks, 8, 128))
    sent = jnp.concatenate(
        [mine[:, None], spread(heads), other[:chips, None], spread(other[chips:])], 1
    )
    came = lax.all_to_all(sent, "col", 0, 0, tiled=True, axis_index_groups=groups)
    came = came.reshape(n_col, 1 + row_blocks, 8, 128)
    col = came[:, 0]
    turned = jnp.concatenate([-col[:, 4:], col[:, :4]], 1)
    right = jnp.concatenate([col, turned], 2).reshape(n_col * 8, 256)
    left = came[:, 1:].transpose(1, 0, 2, 3).reshape(row_blocks, n_col * 8, 128)
    part = -lax.dot_general(
        left, right, (((1,), (0,)), ((), ())), preferred_element_type=F32
    )
    part = part.reshape(n_val, ROW_DEV, 256).astype(BF)
    summands = lax.all_to_all(part, "val", 0, 0, tiled=True)
    total = jnp.sum(summands.astype(F32), 0)
    return total.reshape(ROW_DEV, 2, 128).transpose(1, 0, 2)


def solution(mesh):
    return jax.shard_map(
        local,
        mesh=mesh,
        in_specs=(
            P("val", "col", None, None, None),
            P(),
            P("val"),
            P("col", None, None, None),
            P("col"),
            P(),
        ),
        out_specs=P(None, "val", "col"),
        check_vma=False,
    )
```

```python
import numpy as np

import jax
import jax.numpy as jnp
from jax import lax
from jax.experimental import pallas as pl
from jax.experimental.pallas import tpu as pltpu
from jax.sharding import PartitionSpec as P

ROW_DEV = 64
L = 48
YI = 8
YB = L // YI
SLAB = YI * L
R1 = YB * L
K1 = 6 * L
K2 = 6 * SLAB
ROOT = 0.75 ** 0.5
BF = jnp.bfloat16
F32 = jnp.float32


def tables():
    def trig(phase):
        angle = 2.0 * np.pi * (phase % L) / L
        return np.stack([np.cos(angle), np.sin(angle)]).astype(np.float32)

    r = np.arange(L)
    ka_of = np.repeat(np.arange(YI), L)
    kz_of = np.tile(r, YI)
    t1 = trig(r[:, None] * r[None, :])
    t1 = np.block([[t1[0], t1[1]], [-t1[1], t1[0]]])
    t2a = trig(r[:, None] * kz_of[None, :])
    t2b = trig(6 * np.arange(YI)[:, None] * ka_of[None, :])
    yi_of = np.repeat(np.arange(YI), L)
    tw = trig(np.arange(8)[:, None] * yi_of[None, :])
    return t1, t2a, t2b, tw


def split(value):
    hi = value.astype(BF)
    return hi, (value - hi.astype(F32)).astype(BF)


def dft3(s):
    (r0, i0), (r1, i1), (r2, i2) = s
    tr, ti = r1 + r2, i1 + i2
    ur, ui = r0 - 0.5 * tr, i0 - 0.5 * ti
    dr, di = (r1 - r2) * ROOT, (i1 - i2) * ROOT
    return [(r0 + tr, i0 + ti), (ur + di, ui - dr), (ur - di, ui + dr)]


def dft6(p):
    a = [(p[m][0] + p[m + 3][0], p[m][1] + p[m + 3][1]) for m in range(3)]
    b = [(p[m][0] - p[m + 3][0], p[m][1] - p[m + 3][1]) for m in range(3)]
    b[1] = (p[4][0] - p[1][0], p[4][1] - p[1][1])
    even = dft3(a)
    odd = dft3(b)
    return [even[0], odd[2], even[1], odd[0], even[2], odd[1]]


def fill_tables(t1, t2a, t2b, a1, b2):
    hi, lo = split(t1[...])
    a1[:, 0:2 * L] = hi
    a1[:, 2 * L:4 * L] = lo
    a1[:, 4 * L:6 * L] = hi
    for yi in range(YI):
        cb = t2b[0, yi:yi + 1, :]
        sb = t2b[1, yi:yi + 1, :]
        cos = t2a[0] * cb - t2a[1] * sb
        sin = t2a[1] * cb + t2a[0] * sb
        for value, negative, spots in ((cos, False, ((0, 0), (1, 1))), (sin, True, ((1, 0), (0, 1)))):
            hi, lo = split(value)
            for ri, half in spots:
                flip = negative and ri == 0
                high, low = (-hi, -lo) if flip else (hi, lo)
                cols = slice(half * SLAB, (half + 1) * SLAB)
                r0 = ri * SLAB + yi * L
                b2[r0:r0 + L, cols] = high
                b2[2 * SLAB + r0:2 * SLAB + r0 + L, cols] = low
                b2[4 * SLAB + r0:4 * SLAB + r0 + L, cols] = high


def pairs_kernel(
    word_any, c_any, v_ref, scale_ref, t1, t2a, t2b, tw, hot_ref, out_ref,
    word, c_ref, a1, b2, p3, l2, grid, d0, d1, d2, d3, sems, word_sem,
):
    def fetch(band):
        return pltpu.make_async_copy(c_any.at[band], c_ref.at[band], sems.at[band])

    word_copy = pltpu.make_async_copy(word_any, word, word_sem)
    for band in range(c_any.shape[0]):
        fetch(band).start()
    word_copy.start()
    fill_tables(t1, t2a, t2b, a1, b2)

    def bands(step, carry):
        for bb in range(2):
            fetch(2 * step + bb).wait()
            for lt in range(SLAB // 128):
                for xc in range(L // 16):
                    xs = slice(xc * 16, xc * 16 + 16)
                    cols = slice(bb * SLAB + lt * 128, bb * SLAB + lt * 128 + 128)
                    p = []
                    for yb in range(YB):
                        lanes = slice(yb * SLAB + lt * 128, yb * SLAB + lt * 128 + 128)
                        v0 = v_ref[0, xs, lanes]
                        v1 = v_ref[1, xs, lanes]
                        c0 = c_ref[2 * step + bb, 0, xs, lanes]
                        c1 = c_ref[2 * step + bb, 1, xs, lanes]
                        p.append((v0 * c0 + v1 * c1, v0 * c1 - v1 * c0))
                    for kb, q in enumerate(dft6(p)):
                        for ri in range(2):
                            hi, lo = split(q[ri])
                            r0 = ri * L + xc * 16
                            p3[kb, r0:r0 + 16, cols] = hi
                            p3[kb, 2 * L + r0:2 * L + r0 + 16, cols] = hi
                            p3[kb, 4 * L + r0:4 * L + r0 + 16, cols] = lo
        for kb in range(YB):
            z = jnp.dot(a1[...], p3[kb], preferred_element_type=F32)
            cw = tw[0, kb:kb + 1, :]
            sw = tw[1, kb:kb + 1, :]
            for bb in range(2):
                zr = z[:L, bb * SLAB:(bb + 1) * SLAB]
                zi = z[L:, bb * SLAB:(bb + 1) * SLAB]
                rows = slice(bb * R1 + kb * L, bb * R1 + kb * L + L)
                for ri, value in enumerate((zr * cw + zi * sw, zi * cw - zr * sw)):
                    hi, lo = split(value)
                    l2[rows, ri * SLAB:(ri + 1) * SLAB] = hi
                    l2[rows, (2 + ri) * SLAB:(3 + ri) * SLAB] = hi
                    l2[rows, (4 + ri) * SLAB:(5 + ri) * SLAB] = lo
        y = jnp.dot(l2[...], b2[...], preferred_element_type=F32)
        for bb in range(2):
            scale = scale_ref[pl.ds(2 * step + bb, 1), :]
            for ri in range(2):
                for t in range(3):
                    c0 = ri * SLAB + t * 128
                    start = t * 8 + ri * 4 + bb + 2 * step
                    grid[pl.ds(start, R1, stride=24), :] = y[bb * R1:(bb + 1) * R1, c0:c0 + 128] * scale
        return carry

    lax.fori_loop(0, 2, bands, 0)

    row = lax.broadcasted_iota(jnp.int32, (16, 8 * 128), 0)
    comp = lax.broadcasted_iota(jnp.int32, (16, 8 * 128), 1) // 128
    pick = [(row == comp + 8 * h).astype(F32).astype(BF) for h in range(2)]

    def copy(p, d, first, last):
        for j in range(first, last):
            h, i = divmod(j, 128)
            start = pl.multiple_of(word[p * 256 + j], 8)
            d[h][pl.ds(i // 8 * 64 + i % 8, 8, stride=8), :] = grid[pl.ds(start, 8), :]

    def partial_sum(p, d, k):
        h, c0 = divmod(2 * k, 8)
        hot = hot_ref[p * 256 + h * 128:p * 256 + h * 128 + 128, :]
        rows = []
        for c in (c0, c0 + 1):
            cell = jnp.concatenate([d[h][ib * 64 + c * 8:ib * 64 + c * 8 + 8, :] for ib in range(16)], 0)
            rows.append(cell.astype(BF) * hot)
        return lax.dot_general(
            pick[h][:, c0 * 128:c0 * 128 + 256], jnp.concatenate(rows, 1),
            (((1,), (1,)), ((), ())), preferred_element_type=F32,
        )

    word_copy.wait()
    buffers = (d0, d1), (d2, d3)
    count = out_ref.shape[0] // 16
    copy(0, buffers[0], 0, 256)
    for p in range(count):
        total = None
        for k in range(8):
            got = partial_sum(p, buffers[p % 2], k)
            total = got if total is None else total + got
            if p + 1 < count:
                copy(p + 1, buffers[(p + 1) % 2], 32 * k, 32 * k + 32)
        out_ref[p * 16:p * 16 + 16, :] = total.astype(BF)


def pair_elements(valence, cond, scale, words, hot):
    count = words.shape[0]
    rows = count // 128 * 8
    vmem = pl.BlockSpec(memory_space=pltpu.VMEM)
    hbm = pl.BlockSpec(memory_space=pltpu.HBM)
    cond = pltpu.with_memory_space_constraint(cond, pltpu.HBM)
    return pl.pallas_call(
        pairs_kernel,
        out_shape=jax.ShapeDtypeStruct((rows, 128), BF),
        in_specs=[hbm, hbm] + [vmem] * 7,
        out_specs=vmem,
        scratch_shapes=[
            pltpu.SMEM((count,), jnp.int32),
            pltpu.VMEM(cond.shape, F32),
            pltpu.VMEM((2 * L, K1), BF),
            pltpu.VMEM((K2, 2 * SLAB), BF),
            pltpu.VMEM((YB, K1, 2 * SLAB), BF),
            pltpu.VMEM((2 * R1, K2), BF),
            pltpu.VMEM((R1 * 24, 128), F32),
        ] + [pltpu.VMEM((8 * 128, 128), F32)] * 4 + [
            pltpu.SemaphoreType.DMA((cond.shape[0],)),
            pltpu.SemaphoreType.DMA(()),
        ],
        compiler_params=pltpu.CompilerParams(vmem_limit_bytes=40 << 20),
        name="pairs",
    )(words, cond, valence, scale, *tables(), hot)


def gather_words(gvec_index):
    kx = gvec_index // (L * L)
    ky = gvec_index // L % L
    kz = gvec_index % L
    lane = ky // YB * L + kz
    tile = (ky % YB * L + kx) * 3 + lane // 128
    hot = (lane % 128)[:, None] == lax.iota(jnp.int32, 128)[None, :]
    return tile * 8, hot.astype(F32).astype(BF)


def local(valence_store, band_owner, valence_energy, cond_bands, cond_energy, gvec_index):
    n_col = lax.axis_size("col")
    n_val = lax.axis_size("val")
    chips = n_col // 2
    core = lax.axis_index("col") & 1
    bands = lax.iota(jnp.int32, band_owner.shape[0])
    owner = jnp.sum(jnp.where(bands == lax.axis_index("val"), band_owner, 0))
    spread = jnp.broadcast_to(band_owner[:, None], (band_owner.shape[0], 128))
    owner_core = jnp.sum(jnp.where(bands[:, None] == lax.axis_index("val"), spread, 0), 0) & 1

    tiles = valence_store[0, 0].astype(jnp.float16).reshape(2, 6, 8, 18, 128)
    tiles = tiles.transpose(0, 1, 3, 2, 4).reshape(2, 108, 8, 128)
    tiles = jnp.pad(tiles, ((0, 0), (0, 4), (0, 0), (0, 0)))
    swap = [(i, i ^ 1) for i in range(n_col)]
    mine = lax.dynamic_index_in_dim(tiles, core, 0, False)
    theirs = lax.dynamic_index_in_dim(tiles, 1 - core, 0, False)
    other = lax.ppermute(theirs, "col", swap)
    half = jnp.where(owner_core[None, None, :] == core, mine, other)
    groups = [[q * 2 + c for q in range(chips)] for c in range(2)]
    got = lax.all_to_all(half.reshape(chips, 7, 8, 128), "col", 0, 0, tiled=True, axis_index_groups=groups)
    total_bands = cond_bands.shape[0] * n_col * n_val
    constant = total_bands ** (-0.25) * L ** (-1.5)
    scaling = jnp.sqrt(2.0 / (cond_energy - valence_energy[0])) * constant
    scale = jnp.broadcast_to(scaling[:, None], (scaling.shape[0], 128))
    words, hot = gather_words(gvec_index)
    chunk = lax.dynamic_index_in_dim(got, owner >> 1, 0, True)
    chunk, scale, words, hot = lax.optimization_barrier((chunk, scale, words, hot))
    again = jnp.broadcast_to(chunk, (chips, 7, 8, 128))
    half = lax.all_to_all(again, "col", 0, 0, tiled=True, axis_index_groups=groups).reshape(112, 8, 128)
    other = lax.ppermute(half, "col", swap)
    both = jnp.stack([jnp.where(core == 0, half, other), jnp.where(core == 0, other, half)], 0)
    valence = both[:, :108].reshape(2, 6, 18, 8, 128).transpose(0, 1, 3, 2, 4).reshape(2, L, L * L).astype(F32)

    pairs = pair_elements(valence, cond_bands, scale, words, hot).reshape(n_col, 8, 128)

    row_count = ROW_DEV * n_val
    row_blocks = row_count // 128
    heads = pairs[:row_blocks]
    by_core = pairs.reshape(chips, 2, 8, 128)
    mine = lax.dynamic_index_in_dim(by_core, core, 1, False)
    theirs = lax.dynamic_index_in_dim(by_core, 1 - core, 1, False)
    other = lax.ppermute(jnp.concatenate([theirs, heads], 0), "col", swap)
    spread = lambda block: jnp.broadcast_to(block[None], (chips, row_blocks, 8, 128))
    sent = jnp.concatenate(
        [mine[:, None], spread(heads), other[:chips, None], spread(other[chips:])], 1
    )
    came = lax.all_to_all(sent, "col", 0, 0, tiled=True, axis_index_groups=groups)
    came = came.reshape(n_col, 1 + row_blocks, 8, 128)
    col = came[:, 0]
    turned = jnp.concatenate([-col[:, 4:], col[:, :4]], 1)
    right = jnp.concatenate([col, turned], 2).reshape(n_col * 8, 256)
    left = came[:, 1:].transpose(1, 0, 2, 3).reshape(row_blocks, n_col * 8, 128)
    part = -lax.dot_general(
        left, right, (((1,), (0,)), ((), ())), preferred_element_type=F32
    )
    part = part.reshape(n_val, ROW_DEV, 256).astype(BF)
    summands = lax.all_to_all(part, "val", 0, 0, tiled=True)
    total = jnp.sum(summands.astype(F32), 0)
    return total.reshape(ROW_DEV, 2, 128).transpose(1, 0, 2)


def solution(mesh):
    return jax.shard_map(
        local,
        mesh=mesh,
        in_specs=(
            P("val", "col", None, None, None),
            P(),
            P("val"),
            P("col", None, None, None),
            P("col"),
            P(),
        ),
        out_specs=P(None, "val", "col"),
        check_vma=False,
    )
```

```python
import numpy as np

import jax
import jax.numpy as jnp
from jax import lax
from jax.experimental import pallas as pl
from jax.experimental.pallas import tpu as pltpu
from jax.sharding import PartitionSpec as P

ROW_DEV = 64
L = 48
YI = 8
YB = L // YI
SLAB = YI * L
R1 = YB * L
K1 = 6 * L
K2 = 6 * SLAB
ROOT = 0.75 ** 0.5
BF = jnp.bfloat16
F32 = jnp.float32


def tables():
    def trig(phase):
        angle = 2.0 * np.pi * (phase % L) / L
        return np.stack([np.cos(angle), np.sin(angle)]).astype(np.float32)

    r = np.arange(L)
    ka_of = np.repeat(np.arange(YI), L)
    kz_of = np.tile(r, YI)
    t1 = trig(r[:, None] * r[None, :])
    t1 = np.block([[t1[0], t1[1]], [-t1[1], t1[0]]])
    t2a = trig(r[:, None] * kz_of[None, :])
    t2b = trig(6 * np.arange(YI)[:, None] * ka_of[None, :])
    yi_of = np.repeat(np.arange(YI), L)
    tw = trig(np.arange(8)[:, None] * yi_of[None, :])
    return t1, t2a, t2b, tw


def split(value):
    hi = value.astype(BF)
    return hi, (value - hi.astype(F32)).astype(BF)


def dft3(s):
    (r0, i0), (r1, i1), (r2, i2) = s
    tr, ti = r1 + r2, i1 + i2
    ur, ui = r0 - 0.5 * tr, i0 - 0.5 * ti
    dr, di = (r1 - r2) * ROOT, (i1 - i2) * ROOT
    return [(r0 + tr, i0 + ti), (ur + di, ui - dr), (ur - di, ui + dr)]


def dft6(p):
    a = [(p[m][0] + p[m + 3][0], p[m][1] + p[m + 3][1]) for m in range(3)]
    b = [(p[m][0] - p[m + 3][0], p[m][1] - p[m + 3][1]) for m in range(3)]
    b[1] = (p[4][0] - p[1][0], p[4][1] - p[1][1])
    even = dft3(a)
    odd = dft3(b)
    return [even[0], odd[2], even[1], odd[0], even[2], odd[1]]


def fill_tables(t1, t2a, t2b, a1, b2):
    hi, lo = split(t1[...])
    a1[:, 0:2 * L] = hi
    a1[:, 2 * L:4 * L] = lo
    a1[:, 4 * L:6 * L] = hi
    for yi in range(YI):
        cb = t2b[0, yi:yi + 1, :]
        sb = t2b[1, yi:yi + 1, :]
        cos = t2a[0] * cb - t2a[1] * sb
        sin = t2a[1] * cb + t2a[0] * sb
        for value, negative, spots in ((cos, False, ((0, 0), (1, 1))), (sin, True, ((1, 0), (0, 1)))):
            hi, lo = split(value)
            for ri, half in spots:
                flip = negative and ri == 0
                high, low = (-hi, -lo) if flip else (hi, lo)
                cols = slice(half * SLAB, (half + 1) * SLAB)
                r0 = ri * SLAB + yi * L
                b2[r0:r0 + L, cols] = high
                b2[2 * SLAB + r0:2 * SLAB + r0 + L, cols] = low
                b2[4 * SLAB + r0:4 * SLAB + r0 + L, cols] = high


def pairs_kernel(
    word_any, c_any, v_ref, scale_ref, t1, t2a, t2b, tw, spot_ref, out_ref,
    word, c_ref, a1, b2, p3, l2, grid, d0, d1, d2, d3, sems, word_sem,
):
    def fetch(band):
        return pltpu.make_async_copy(c_any.at[band], c_ref.at[band], sems.at[band])

    word_copy = pltpu.make_async_copy(word_any, word, word_sem)
    for band in range(c_any.shape[0]):
        fetch(band).start()
    word_copy.start()
    fill_tables(t1, t2a, t2b, a1, b2)

    def bands(step, carry):
        for bb in range(2):
            fetch(2 * step + bb).wait()
            for lt in range(SLAB // 128):
                for xc in range(L // 16):
                    xs = slice(xc * 16, xc * 16 + 16)
                    cols = slice(bb * SLAB + lt * 128, bb * SLAB + lt * 128 + 128)
                    p = []
                    for yb in range(YB):
                        lanes = slice(yb * SLAB + lt * 128, yb * SLAB + lt * 128 + 128)
                        v0 = v_ref[0, xs, lanes]
                        v1 = v_ref[1, xs, lanes]
                        c0 = c_ref[2 * step + bb, 0, xs, lanes]
                        c1 = c_ref[2 * step + bb, 1, xs, lanes]
                        p.append((v0 * c0 + v1 * c1, v0 * c1 - v1 * c0))
                    for kb, q in enumerate(dft6(p)):
                        for ri in range(2):
                            hi, lo = split(q[ri])
                            r0 = ri * L + xc * 16
                            p3[kb, r0:r0 + 16, cols] = hi
                            p3[kb, 2 * L + r0:2 * L + r0 + 16, cols] = hi
                            p3[kb, 4 * L + r0:4 * L + r0 + 16, cols] = lo
        for kb in range(YB):
            z = jnp.dot(a1[...], p3[kb], preferred_element_type=F32)
            cw = tw[0, kb:kb + 1, :]
            sw = tw[1, kb:kb + 1, :]
            for bb in range(2):
                zr = z[:L, bb * SLAB:(bb + 1) * SLAB]
                zi = z[L:, bb * SLAB:(bb + 1) * SLAB]
                rows = slice(bb * R1 + kb * L, bb * R1 + kb * L + L)
                for ri, value in enumerate((zr * cw + zi * sw, zi * cw - zr * sw)):
                    hi, lo = split(value)
                    l2[rows, ri * SLAB:(ri + 1) * SLAB] = hi
                    l2[rows, (2 + ri) * SLAB:(3 + ri) * SLAB] = hi
                    l2[rows, (4 + ri) * SLAB:(5 + ri) * SLAB] = lo
        y = jnp.dot(l2[...], b2[...], preferred_element_type=F32)
        for bb in range(2):
            scale = scale_ref[pl.ds(2 * step + bb, 1), :]
            for ri in range(2):
                for t in range(3):
                    c0 = ri * SLAB + t * 128
                    start = t * 8 + ri * 4 + bb + 2 * step
                    grid[pl.ds(start, R1, stride=24), :] = y[bb * R1:(bb + 1) * R1, c0:c0 + 128] * scale
        return carry

    lax.fori_loop(0, 2, bands, 0)

    row = lax.broadcasted_iota(jnp.int32, (16, 8 * 128), 0)
    comp = lax.broadcasted_iota(jnp.int32, (16, 8 * 128), 1) // 128
    pick = [(row == comp + 8 * h).astype(F32).astype(BF) for h in range(2)]

    def copy(p, d, first, last):
        for j in range(first, last):
            h, i = divmod(j, 128)
            start = pl.multiple_of(word[p * 256 + j], 8)
            d[h][pl.ds(i // 8 * 64 + i % 8, 8, stride=8), :] = grid[pl.ds(start, 8), :]

    lane = lax.broadcasted_iota(jnp.int32, (128, 128), 1).astype(F32)

    def one_hot(b):
        spots = jnp.broadcast_to(spot_ref[b:b + 1, :], (128, 128)).T
        return (spots == lane).astype(F32).astype(BF)

    def partial_sum(p, d, k, hot):
        h, c0 = divmod(2 * k, 8)
        rows = []
        for c in (c0, c0 + 1):
            cell = jnp.concatenate([d[h][ib * 64 + c * 8:ib * 64 + c * 8 + 8, :] for ib in range(16)], 0)
            rows.append(cell.astype(BF) * hot)
        return lax.dot_general(
            pick[h][:, c0 * 128:c0 * 128 + 256], jnp.concatenate(rows, 1),
            (((1,), (1,)), ((), ())), preferred_element_type=F32,
        )

    word_copy.wait()
    buffers = (d0, d1), (d2, d3)
    count = out_ref.shape[0] // 16
    copy(0, buffers[0], 0, 256)
    for p in range(count):
        total = None
        for k in range(8):
            if k % 4 == 0:
                hot = one_hot(2 * p + k // 4)
            got = partial_sum(p, buffers[p % 2], k, hot)
            total = got if total is None else total + got
            if p + 1 < count:
                copy(p + 1, buffers[(p + 1) % 2], 32 * k, 32 * k + 32)
        out_ref[p * 16:p * 16 + 16, :] = total.astype(BF)


def pair_elements(valence, cond, scale, words, spots):
    count = words.shape[0]
    rows = count // 128 * 8
    vmem = pl.BlockSpec(memory_space=pltpu.VMEM)
    hbm = pl.BlockSpec(memory_space=pltpu.HBM)
    cond = pltpu.with_memory_space_constraint(cond, pltpu.HBM)
    return pl.pallas_call(
        pairs_kernel,
        out_shape=jax.ShapeDtypeStruct((rows, 128), BF),
        in_specs=[hbm, hbm] + [vmem] * 7,
        out_specs=vmem,
        scratch_shapes=[
            pltpu.SMEM((count,), jnp.int32),
            pltpu.VMEM(cond.shape, F32),
            pltpu.VMEM((2 * L, K1), BF),
            pltpu.VMEM((K2, 2 * SLAB), BF),
            pltpu.VMEM((YB, K1, 2 * SLAB), BF),
            pltpu.VMEM((2 * R1, K2), BF),
            pltpu.VMEM((R1 * 24, 128), F32),
        ] + [pltpu.VMEM((8 * 128, 128), F32)] * 4 + [
            pltpu.SemaphoreType.DMA((cond.shape[0],)),
            pltpu.SemaphoreType.DMA(()),
        ],
        compiler_params=pltpu.CompilerParams(vmem_limit_bytes=40 << 20),
        name="pairs",
    )(words, cond, valence, scale, *tables(), spots)


def gather_words(gvec_index):
    kx = gvec_index // (L * L)
    ky = gvec_index // L % L
    kz = gvec_index % L
    lane = ky // YB * L + kz
    tile = (ky % YB * L + kx) * 3 + lane // 128
    return tile * 8, (lane % 128).astype(F32).reshape(-1, 128)


def local(valence_store, band_owner, valence_energy, cond_bands, cond_energy, gvec_index):
    n_col = lax.axis_size("col")
    n_val = lax.axis_size("val")
    chips = n_col // 2
    core = lax.axis_index("col") & 1
    bands = lax.iota(jnp.int32, band_owner.shape[0])
    spread = jnp.broadcast_to(band_owner[:, None], (band_owner.shape[0], 128))
    owner = jnp.sum(jnp.where(bands[:, None] == lax.axis_index("val"), spread, 0), 0)

    tiles = valence_store[0, 0].astype(jnp.float16).reshape(2, 6, 8, 18, 128)
    tiles = tiles.transpose(0, 1, 3, 2, 4).reshape(2, 108, 8, 128)
    tiles = jnp.pad(tiles, ((0, 0), (0, 4), (0, 0), (0, 0)))
    swap = [(i, i ^ 1) for i in range(n_col)]
    mine = lax.dynamic_index_in_dim(tiles, core, 0, False)
    theirs = lax.dynamic_index_in_dim(tiles, 1 - core, 0, False)
    other = lax.ppermute(theirs, "col", swap)
    half = jnp.where((owner & 1)[None, None, :] == core, mine, other)
    source = lax.iota(jnp.int32, chips)[:, None] == (owner >> 1)[None, :]
    half, words, spots, source = lax.optimization_barrier((half, *gather_words(gvec_index), source))
    groups = [[q * 2 + c for q in range(chips)] for c in range(2)]
    got = lax.all_to_all(half.reshape(chips, 7, 8, 128), "col", 0, 0, tiled=True, axis_index_groups=groups)
    chunk = jnp.sum(jnp.where(source[:, None, None, :], got, 0).astype(F32), 0, keepdims=True)
    again = jnp.broadcast_to(chunk.astype(got.dtype), (chips, 7, 8, 128))
    half = lax.all_to_all(again, "col", 0, 0, tiled=True, axis_index_groups=groups).reshape(112, 8, 128)
    half, cond_energy, valence_energy = lax.optimization_barrier((half, cond_energy, valence_energy))
    other = lax.ppermute(half, "col", swap)
    both = jnp.stack([jnp.where(core == 0, half, other), jnp.where(core == 0, other, half)], 0)
    valence = both[:, :108].reshape(2, 6, 18, 8, 128).transpose(0, 1, 3, 2, 4).reshape(2, L, L * L).astype(F32)

    total_bands = cond_bands.shape[0] * n_col * n_val
    constant = total_bands ** (-0.25) * L ** (-1.5)
    scaling = jnp.sqrt(2.0 / (cond_energy - valence_energy[0])) * constant
    scale = jnp.broadcast_to(scaling[:, None], (scaling.shape[0], 128))
    pairs = pair_elements(valence, cond_bands, scale, words, spots).reshape(n_col, 8, 128)

    row_count = ROW_DEV * n_val
    row_blocks = row_count // 128
    heads = pairs[:row_blocks]
    by_core = pairs.reshape(chips, 2, 8, 128)
    mine = lax.dynamic_index_in_dim(by_core, core, 1, False)
    theirs = lax.dynamic_index_in_dim(by_core, 1 - core, 1, False)
    other = lax.ppermute(jnp.concatenate([theirs, heads], 0), "col", swap)
    spread = lambda block: jnp.broadcast_to(block[None], (chips, row_blocks, 8, 128))
    sent = jnp.concatenate(
        [mine[:, None], spread(heads), other[:chips, None], spread(other[chips:])], 1
    )
    came = lax.all_to_all(sent, "col", 0, 0, tiled=True, axis_index_groups=groups)
    came = came.reshape(n_col, 1 + row_blocks, 8, 128)
    col = came[:, 0]
    turned = jnp.concatenate([-col[:, 4:], col[:, :4]], 1)
    right = jnp.concatenate([col, turned], 2).reshape(n_col * 8, 256)
    left = came[:, 1:].transpose(1, 0, 2, 3).reshape(row_blocks, n_col * 8, 128)
    part = -lax.dot_general(
        left, right, (((1,), (0,)), ((), ())), preferred_element_type=F32
    )
    part = part.reshape(n_val, ROW_DEV, 256).astype(BF)
    summands = lax.all_to_all(part, "val", 0, 0, tiled=True)
    total = jnp.sum(summands.astype(F32), 0)
    return total.reshape(ROW_DEV, 2, 128).transpose(1, 0, 2)


def solution(mesh):
    return jax.shard_map(
        local,
        mesh=mesh,
        in_specs=(
            P("val", "col", None, None, None),
            P(),
            P("val"),
            P("col", None, None, None),
            P("col"),
            P(),
        ),
        out_specs=P(None, "val", "col"),
        check_vma=False,
    )
```

```python
import numpy as np

import jax
import jax.numpy as jnp
from jax import lax
from jax.experimental import pallas as pl
from jax.experimental.pallas import tpu as pltpu
from jax.sharding import PartitionSpec as P

ROW_DEV = 64
L = 48
YI = 8
YB = L // YI
SLAB = YI * L
R1 = YB * L
K1 = 6 * L
K2 = 6 * SLAB
ROOT = 0.75 ** 0.5
BF = jnp.bfloat16
F32 = jnp.float32


def tables():
    def trig(phase):
        angle = 2.0 * np.pi * (phase % L) / L
        return np.stack([np.cos(angle), np.sin(angle)]).astype(np.float32)

    r = np.arange(L)
    ka_of = np.repeat(np.arange(YI), L)
    kz_of = np.tile(r, YI)
    t1 = trig(r[:, None] * r[None, :])
    t1 = np.block([[t1[0], t1[1]], [-t1[1], t1[0]]])
    t2a = trig(r[:, None] * kz_of[None, :])
    t2b = trig(6 * np.arange(YI)[:, None] * ka_of[None, :])
    yi_of = np.repeat(np.arange(YI), L)
    tw = trig(np.arange(8)[:, None] * yi_of[None, :])
    return t1, t2a, t2b, tw


def split(value):
    hi = value.astype(BF)
    return hi, (value - hi.astype(F32)).astype(BF)


def dft3(s):
    (r0, i0), (r1, i1), (r2, i2) = s
    tr, ti = r1 + r2, i1 + i2
    ur, ui = r0 - 0.5 * tr, i0 - 0.5 * ti
    dr, di = (r1 - r2) * ROOT, (i1 - i2) * ROOT
    return [(r0 + tr, i0 + ti), (ur + di, ui - dr), (ur - di, ui + dr)]


def dft6(p):
    a = [(p[m][0] + p[m + 3][0], p[m][1] + p[m + 3][1]) for m in range(3)]
    b = [(p[m][0] - p[m + 3][0], p[m][1] - p[m + 3][1]) for m in range(3)]
    b[1] = (p[4][0] - p[1][0], p[4][1] - p[1][1])
    even = dft3(a)
    odd = dft3(b)
    return [even[0], odd[2], even[1], odd[0], even[2], odd[1]]


def fill_tables(t1, t2a, t2b, a1, b2):
    hi, lo = split(t1[...])
    a1[:, 0:2 * L] = hi
    a1[:, 2 * L:4 * L] = lo
    a1[:, 4 * L:6 * L] = hi
    for yi in range(YI):
        cb = t2b[0, yi:yi + 1, :]
        sb = t2b[1, yi:yi + 1, :]
        cos = t2a[0] * cb - t2a[1] * sb
        sin = t2a[1] * cb + t2a[0] * sb
        for value, negative, spots in ((cos, False, ((0, 0), (1, 1))), (sin, True, ((1, 0), (0, 1)))):
            hi, lo = split(value)
            for ri, half in spots:
                flip = negative and ri == 0
                high, low = (-hi, -lo) if flip else (hi, lo)
                cols = slice(half * SLAB, (half + 1) * SLAB)
                r0 = ri * SLAB + yi * L
                b2[r0:r0 + L, cols] = high
                b2[2 * SLAB + r0:2 * SLAB + r0 + L, cols] = low
                b2[4 * SLAB + r0:4 * SLAB + r0 + L, cols] = high


def pairs_kernel(
    word_any, c_any, v_ref, scale_ref, t1, t2a, t2b, tw, spot_ref, out_ref,
    word, c_ref, a1, b2, p3, l2, grid, d0, d1, d2, d3, sems, word_sem,
):
    def fetch(band):
        return pltpu.make_async_copy(c_any.at[band], c_ref.at[band], sems.at[band])

    word_copy = pltpu.make_async_copy(word_any, word, word_sem)
    for band in range(c_any.shape[0]):
        fetch(band).start()
    word_copy.start()
    fill_tables(t1, t2a, t2b, a1, b2)

    def bands(step, carry):
        for bb in range(2):
            fetch(2 * step + bb).wait()
            for lt in range(SLAB // 128):
                for xc in range(L // 16):
                    xs = slice(xc * 16, xc * 16 + 16)
                    cols = slice(bb * SLAB + lt * 128, bb * SLAB + lt * 128 + 128)
                    p = []
                    for yb in range(YB):
                        lanes = slice(yb * SLAB + lt * 128, yb * SLAB + lt * 128 + 128)
                        v0 = v_ref[0, xs, lanes]
                        v1 = v_ref[1, xs, lanes]
                        c0 = c_ref[2 * step + bb, 0, xs, lanes]
                        c1 = c_ref[2 * step + bb, 1, xs, lanes]
                        p.append((v0 * c0 + v1 * c1, v0 * c1 - v1 * c0))
                    for kb, q in enumerate(dft6(p)):
                        for ri in range(2):
                            hi, lo = split(q[ri])
                            r0 = ri * L + xc * 16
                            p3[kb, r0:r0 + 16, cols] = hi
                            p3[kb, 2 * L + r0:2 * L + r0 + 16, cols] = hi
                            p3[kb, 4 * L + r0:4 * L + r0 + 16, cols] = lo
        for kb in range(YB):
            z = jnp.dot(a1[...], p3[kb], preferred_element_type=F32)
            cw = tw[0, kb:kb + 1, :]
            sw = tw[1, kb:kb + 1, :]
            for bb in range(2):
                zr = z[:L, bb * SLAB:(bb + 1) * SLAB]
                zi = z[L:, bb * SLAB:(bb + 1) * SLAB]
                rows = slice(bb * R1 + kb * L, bb * R1 + kb * L + L)
                for ri, value in enumerate((zr * cw + zi * sw, zi * cw - zr * sw)):
                    hi, lo = split(value)
                    l2[rows, ri * SLAB:(ri + 1) * SLAB] = hi
                    l2[rows, (2 + ri) * SLAB:(3 + ri) * SLAB] = hi
                    l2[rows, (4 + ri) * SLAB:(5 + ri) * SLAB] = lo
        y = jnp.dot(l2[...], b2[...], preferred_element_type=F32)
        for bb in range(2):
            scale = scale_ref[pl.ds(2 * step + bb, 1), :]
            for ri in range(2):
                for t in range(3):
                    c0 = ri * SLAB + t * 128
                    start = t * 8 + ri * 4 + bb + 2 * step
                    grid[pl.ds(start, R1, stride=24), :] = y[bb * R1:(bb + 1) * R1, c0:c0 + 128] * scale
        return carry

    lax.fori_loop(0, 2, bands, 0)

    row = lax.broadcasted_iota(jnp.int32, (16, 8 * 128), 0)
    comp = lax.broadcasted_iota(jnp.int32, (16, 8 * 128), 1) // 128
    pick = [(row == comp + 8 * h).astype(F32).astype(BF) for h in range(2)]

    def copy(p, d, first, last):
        for j in range(first, last):
            h, i = divmod(j, 128)
            start = pl.multiple_of(word[p * 256 + j], 8)
            d[h][pl.ds(i // 8 * 64 + i % 8, 8, stride=8), :] = grid[pl.ds(start, 8), :]

    lane = lax.broadcasted_iota(jnp.int32, (128, 128), 1).astype(F32)

    def one_hot(b):
        spots = jnp.broadcast_to(spot_ref[b:b + 1, :], (128, 128)).T
        return (spots == lane).astype(F32).astype(BF)

    def partial_sum(p, d, k, hot):
        h, c0 = divmod(2 * k, 8)
        rows = []
        for c in (c0, c0 + 1):
            cell = jnp.concatenate([d[h][ib * 64 + c * 8:ib * 64 + c * 8 + 8, :] for ib in range(16)], 0)
            rows.append(cell.astype(BF) * hot)
        return lax.dot_general(
            pick[h][:, c0 * 128:c0 * 128 + 256], jnp.concatenate(rows, 1),
            (((1,), (1,)), ((), ())), preferred_element_type=F32,
        )

    word_copy.wait()
    buffers = (d0, d1), (d2, d3)
    count = out_ref.shape[0] // 16
    copy(0, buffers[0], 0, 256)
    for p in range(count):
        total = None
        for k in range(8):
            if k % 4 == 0:
                hot = one_hot(2 * p + k // 4)
            got = partial_sum(p, buffers[p % 2], k, hot)
            total = got if total is None else total + got
            if p + 1 < count:
                copy(p + 1, buffers[(p + 1) % 2], 32 * k, 32 * k + 32)
        out_ref[p * 16:p * 16 + 16, :] = total.astype(BF)


def pair_elements(valence, cond, scale, words, spots):
    count = words.shape[0]
    rows = count // 128 * 8
    vmem = pl.BlockSpec(memory_space=pltpu.VMEM)
    hbm = pl.BlockSpec(memory_space=pltpu.HBM)
    cond = pltpu.with_memory_space_constraint(cond, pltpu.HBM)
    return pl.pallas_call(
        pairs_kernel,
        out_shape=jax.ShapeDtypeStruct((rows, 128), BF),
        in_specs=[hbm, hbm] + [vmem] * 7,
        out_specs=vmem,
        scratch_shapes=[
            pltpu.SMEM((count,), jnp.int32),
            pltpu.VMEM(cond.shape, F32),
            pltpu.VMEM((2 * L, K1), BF),
            pltpu.VMEM((K2, 2 * SLAB), BF),
            pltpu.VMEM((YB, K1, 2 * SLAB), BF),
            pltpu.VMEM((2 * R1, K2), BF),
            pltpu.VMEM((R1 * 24, 128), F32),
        ] + [pltpu.VMEM((8 * 128, 128), F32)] * 4 + [
            pltpu.SemaphoreType.DMA((cond.shape[0],)),
            pltpu.SemaphoreType.DMA(()),
        ],
        compiler_params=pltpu.CompilerParams(vmem_limit_bytes=40 << 20),
        name="pairs",
    )(words, cond, valence, scale, *tables(), spots)


def gather_words(gvec_index):
    kx = gvec_index // (L * L)
    ky = gvec_index // L % L
    kz = gvec_index % L
    lane = ky // YB * L + kz
    tile = (ky % YB * L + kx) * 3 + lane // 128
    return tile * 8, (lane % 128).astype(F32).reshape(-1, 128)


def local(valence_store, band_owner, valence_energy, cond_bands, cond_energy, gvec_index):
    n_col = lax.axis_size("col")
    n_val = lax.axis_size("val")
    chips = n_col // 2
    core = lax.axis_index("col") & 1
    bands = lax.iota(jnp.int32, band_owner.shape[0])
    spread = jnp.broadcast_to(band_owner[:, None], (band_owner.shape[0], 128))
    owner = jnp.sum(jnp.where(bands[:, None] == lax.axis_index("val"), spread, 0), 0)

    def component(field, index):
        tiles = field.reshape(2, 6, 8, 18, 128).transpose(0, 1, 3, 2, 4).reshape(2, 108, 8, 128)
        picked = lax.dynamic_index_in_dim(tiles, index, 0, False).astype(jnp.float16)
        return jnp.pad(picked, ((0, 4), (0, 0), (0, 0)))

    swap = [(i, i ^ 1) for i in range(n_col)]
    theirs = component(valence_store[0, 0], 1 - core)
    other = lax.ppermute(theirs, "col", swap)
    mine = lax.optimization_barrier(component(lax.optimization_barrier(valence_store)[0, 0], core))
    half = jnp.where((owner & 1)[None, None, :] == core, mine, other)
    source = lax.iota(jnp.int32, chips)[:, None] == (owner >> 1)[None, :]
    half, source = lax.optimization_barrier((half, source))
    groups = [[q * 2 + c for q in range(chips)] for c in range(2)]
    got = lax.all_to_all(half.reshape(chips, 7, 8, 128), "col", 0, 0, tiled=True, axis_index_groups=groups)
    got, gvec_index = lax.optimization_barrier((got, gvec_index))
    words, spots = gather_words(gvec_index)
    chunk = jnp.sum(jnp.where(source[:, None, None, :], got, 0).astype(F32), 0, keepdims=True)
    again = jnp.broadcast_to(chunk.astype(got.dtype), (chips, 7, 8, 128))
    again, words, spots = lax.optimization_barrier((again, words, spots))
    half = lax.all_to_all(again, "col", 0, 0, tiled=True, axis_index_groups=groups).reshape(112, 8, 128)
    half, cond_energy, valence_energy = lax.optimization_barrier((half, cond_energy, valence_energy))
    other = lax.ppermute(half, "col", swap)
    both = jnp.stack([jnp.where(core == 0, half, other), jnp.where(core == 0, other, half)], 0)
    valence = both[:, :108].reshape(2, 6, 18, 8, 128).transpose(0, 1, 3, 2, 4).reshape(2, L, L * L).astype(F32)

    total_bands = cond_bands.shape[0] * n_col * n_val
    constant = total_bands ** (-0.25) * L ** (-1.5)
    scaling = jnp.sqrt(2.0 / (cond_energy - valence_energy[0])) * constant
    scale = jnp.broadcast_to(scaling[:, None], (scaling.shape[0], 128))
    pairs = pair_elements(valence, cond_bands, scale, words, spots).reshape(n_col, 8, 128)

    row_count = ROW_DEV * n_val
    row_blocks = row_count // 128
    heads = pairs[:row_blocks]
    by_core = pairs.reshape(chips, 2, 8, 128)
    mine = lax.dynamic_index_in_dim(by_core, core, 1, False)
    theirs = lax.dynamic_index_in_dim(by_core, 1 - core, 1, False)
    other = lax.ppermute(jnp.concatenate([theirs, heads], 0), "col", swap)
    spread = lambda block: jnp.broadcast_to(block[None], (chips, row_blocks, 8, 128))
    sent = jnp.concatenate(
        [mine[:, None], spread(heads), other[:chips, None], spread(other[chips:])], 1
    )
    came = lax.all_to_all(sent, "col", 0, 0, tiled=True, axis_index_groups=groups)
    came = came.reshape(n_col, 1 + row_blocks, 8, 128)
    col = came[:, 0]
    turned = jnp.concatenate([-col[:, 4:], col[:, :4]], 1)
    right = jnp.concatenate([col, turned], 2).reshape(n_col * 8, 256)
    left = came[:, 1:].transpose(1, 0, 2, 3).reshape(row_blocks, n_col * 8, 128)
    part = -lax.dot_general(
        left, right, (((1,), (0,)), ((), ())), preferred_element_type=F32
    )
    part = part.reshape(n_val, ROW_DEV, 256).astype(BF)
    summands = lax.all_to_all(part, "val", 0, 0, tiled=True)
    total = jnp.sum(summands.astype(F32), 0)
    return total.reshape(ROW_DEV, 2, 128).transpose(1, 0, 2)


def solution(mesh):
    return jax.shard_map(
        local,
        mesh=mesh,
        in_specs=(
            P("val", "col", None, None, None),
            P(),
            P("val"),
            P("col", None, None, None),
            P("col"),
            P(),
        ),
        out_specs=P(None, "val", "col"),
        check_vma=False,
    )
```

```python
import numpy as np

import jax
import jax.numpy as jnp
from jax import lax
from jax.experimental import pallas as pl
from jax.experimental.pallas import tpu as pltpu
from jax.sharding import PartitionSpec as P

ROW_DEV = 64
L = 48
YI = 8
YB = L // YI
SLAB = YI * L
R1 = YB * L
K1 = 6 * L
K2 = 6 * SLAB
ROOT = 0.75 ** 0.5
BF = jnp.bfloat16
F32 = jnp.float32


def tables():
    def trig(phase):
        angle = 2.0 * np.pi * (phase % L) / L
        return np.stack([np.cos(angle), np.sin(angle)]).astype(np.float32)

    r = np.arange(L)
    ka_of = np.repeat(np.arange(YI), L)
    kz_of = np.tile(r, YI)
    t1 = trig(r[:, None] * r[None, :])
    t1 = np.block([[t1[0], t1[1]], [-t1[1], t1[0]]])
    t2a = trig(r[:, None] * kz_of[None, :])
    t2b = trig(6 * np.arange(YI)[:, None] * ka_of[None, :])
    yi_of = np.repeat(np.arange(YI), L)
    tw = trig(np.arange(8)[:, None] * yi_of[None, :])
    return t1, t2a, t2b, tw


def split(value):
    hi = value.astype(BF)
    return hi, (value - hi.astype(F32)).astype(BF)


def dft3(s):
    (r0, i0), (r1, i1), (r2, i2) = s
    tr, ti = r1 + r2, i1 + i2
    ur, ui = r0 - 0.5 * tr, i0 - 0.5 * ti
    dr, di = (r1 - r2) * ROOT, (i1 - i2) * ROOT
    return [(r0 + tr, i0 + ti), (ur + di, ui - dr), (ur - di, ui + dr)]


def dft6(p):
    a = [(p[m][0] + p[m + 3][0], p[m][1] + p[m + 3][1]) for m in range(3)]
    b = [(p[m][0] - p[m + 3][0], p[m][1] - p[m + 3][1]) for m in range(3)]
    b[1] = (p[4][0] - p[1][0], p[4][1] - p[1][1])
    even = dft3(a)
    odd = dft3(b)
    return [even[0], odd[2], even[1], odd[0], even[2], odd[1]]


def fill_tables(t1, t2a, t2b, a1, b2):
    hi, lo = split(t1[...])
    a1[:, 0:2 * L] = hi
    a1[:, 2 * L:4 * L] = lo
    a1[:, 4 * L:6 * L] = hi
    for yi in range(YI):
        cb = t2b[0, yi:yi + 1, :]
        sb = t2b[1, yi:yi + 1, :]
        cos = t2a[0] * cb - t2a[1] * sb
        sin = t2a[1] * cb + t2a[0] * sb
        for value, negative, spots in ((cos, False, ((0, 0), (1, 1))), (sin, True, ((1, 0), (0, 1)))):
            hi, lo = split(value)
            for ri, half in spots:
                flip = negative and ri == 0
                high, low = (-hi, -lo) if flip else (hi, lo)
                cols = slice(half * SLAB, (half + 1) * SLAB)
                r0 = ri * SLAB + yi * L
                b2[r0:r0 + L, cols] = high
                b2[2 * SLAB + r0:2 * SLAB + r0 + L, cols] = low
                b2[4 * SLAB + r0:4 * SLAB + r0 + L, cols] = high


def pairs_kernel(
    word_any, c_any, v_ref, scale_ref, t1, t2a, t2b, tw, spot_ref, out_ref,
    word, c_ref, a1, b2, p3, l2, grid, hots, wide, sems, word_sem,
):
    def fetch(band):
        return pltpu.make_async_copy(c_any.at[band], c_ref.at[band], sems.at[band])

    word_copy = pltpu.make_async_copy(word_any, word, word_sem)
    for band in range(c_any.shape[0]):
        fetch(band).start()
    word_copy.start()
    fill_tables(t1, t2a, t2b, a1, b2)

    def bands(step, carry):
        for bb in range(2):
            fetch(2 * step + bb).wait()
            for lt in range(SLAB // 128):
                for xc in range(L // 16):
                    xs = slice(xc * 16, xc * 16 + 16)
                    cols = slice(bb * SLAB + lt * 128, bb * SLAB + lt * 128 + 128)
                    p = []
                    for yb in range(YB):
                        lanes = slice(yb * SLAB + lt * 128, yb * SLAB + lt * 128 + 128)
                        v0 = v_ref[0, xs, lanes]
                        v1 = v_ref[1, xs, lanes]
                        c0 = c_ref[2 * step + bb, 0, xs, lanes]
                        c1 = c_ref[2 * step + bb, 1, xs, lanes]
                        p.append((v0 * c0 + v1 * c1, v0 * c1 - v1 * c0))
                    for kb, q in enumerate(dft6(p)):
                        for ri in range(2):
                            hi, lo = split(q[ri])
                            r0 = ri * L + xc * 16
                            p3[kb, r0:r0 + 16, cols] = hi
                            p3[kb, 2 * L + r0:2 * L + r0 + 16, cols] = hi
                            p3[kb, 4 * L + r0:4 * L + r0 + 16, cols] = lo
        for kb in range(YB):
            z = jnp.dot(a1[...], p3[kb], preferred_element_type=F32)
            cw = tw[0, kb:kb + 1, :]
            sw = tw[1, kb:kb + 1, :]
            for bb in range(2):
                zr = z[:L, bb * SLAB:(bb + 1) * SLAB]
                zi = z[L:, bb * SLAB:(bb + 1) * SLAB]
                rows = slice(bb * R1 + kb * L, bb * R1 + kb * L + L)
                for ri, value in enumerate((zr * cw + zi * sw, zi * cw - zr * sw)):
                    hi, lo = split(value)
                    l2[rows, ri * SLAB:(ri + 1) * SLAB] = hi
                    l2[rows, (2 + ri) * SLAB:(3 + ri) * SLAB] = hi
                    l2[rows, (4 + ri) * SLAB:(5 + ri) * SLAB] = lo
        y = jnp.dot(l2[...], b2[...], preferred_element_type=F32)
        for bb in range(2):
            scale = scale_ref[pl.ds(2 * step + bb, 1), :]
            for ri in range(2):
                for t in range(3):
                    c0 = ri * SLAB + t * 128
                    start = t * 8 + ri * 4 + bb + 2 * step
                    grid[pl.ds(start, R1, stride=24), :] = y[bb * R1:(bb + 1) * R1, c0:c0 + 128] * scale
        return carry

    lax.fori_loop(0, 2, bands, 0)

    lane = lax.broadcasted_iota(jnp.int32, (128, 128), 1).astype(F32)
    own = lax.broadcasted_iota(jnp.int32, (8, 256), 1) % 8 == lax.broadcasted_iota(jnp.int32, (8, 256), 0)
    ones = jnp.ones((16, 128), BF)

    word_copy.wait()
    for b in range(spot_ref.shape[0]):
        hot = hots.at[b % 2]
        hot[...] = (jnp.broadcast_to(spot_ref[b:b + 1, :], (128, 128)).T == lane).astype(F32)
        for j in range(4):
            rows = []
            for i in range(32 * j, 32 * j + 32):
                start = pl.multiple_of(word[b * 128 + i], 8)
                rows.append(grid[pl.ds(start, 8), :] * jnp.broadcast_to(hot[i:i + 1, :], (8, 128)))
            sums = lax.dot_general(
                ones, jnp.concatenate(rows, 0).astype(BF),
                (((1,), (1,)), ((), ())), preferred_element_type=F32,
            )
            wide[b * 8:b * 8 + 8, j * 256:j * 256 + 256] = jnp.where(own, sums[:8], 0.0)
    fold = (
        lax.broadcasted_iota(jnp.int32, (1024, 128), 0) // 8
        == lax.broadcasted_iota(jnp.int32, (1024, 128), 1)
    ).astype(F32).astype(BF)
    out_ref[...] = jnp.dot(wide[...].astype(BF), fold, preferred_element_type=F32).astype(BF)


def pair_elements(valence, cond, scale, words, spots):
    count = words.shape[0]
    rows = count // 128 * 8
    vmem = pl.BlockSpec(memory_space=pltpu.VMEM)
    hbm = pl.BlockSpec(memory_space=pltpu.HBM)
    cond = pltpu.with_memory_space_constraint(cond, pltpu.HBM)
    return pl.pallas_call(
        pairs_kernel,
        out_shape=jax.ShapeDtypeStruct((rows, 128), BF),
        in_specs=[hbm, hbm] + [vmem] * 7,
        out_specs=vmem,
        scratch_shapes=[
            pltpu.SMEM((count,), jnp.int32),
            pltpu.VMEM(cond.shape, F32),
            pltpu.VMEM((2 * L, K1), BF),
            pltpu.VMEM((K2, 2 * SLAB), BF),
            pltpu.VMEM((YB, K1, 2 * SLAB), BF),
            pltpu.VMEM((2 * R1, K2), BF),
            pltpu.VMEM((R1 * 24, 128), F32),
            pltpu.VMEM((2, 128, 128), F32),
            pltpu.VMEM((rows, 1024), F32),
            pltpu.SemaphoreType.DMA((cond.shape[0],)),
            pltpu.SemaphoreType.DMA(()),
        ],
        compiler_params=pltpu.CompilerParams(vmem_limit_bytes=40 << 20),
        name="pairs",
    )(words, cond, valence, scale, *tables(), spots)


def gather_words(gvec_index):
    kx = gvec_index // (L * L)
    ky = gvec_index // L % L
    kz = gvec_index % L
    lane = ky // YB * L + kz
    tile = (ky % YB * L + kx) * 3 + lane // 128
    return tile * 8, (lane % 128).astype(F32).reshape(-1, 128)


def local(valence_store, band_owner, valence_energy, cond_bands, cond_energy, gvec_index):
    n_col = lax.axis_size("col")
    n_val = lax.axis_size("val")
    chips = n_col // 2
    core = lax.axis_index("col") & 1
    bands = lax.iota(jnp.int32, band_owner.shape[0])
    spread = jnp.broadcast_to(band_owner[:, None], (band_owner.shape[0], 128))
    owner = jnp.sum(jnp.where(bands[:, None] == lax.axis_index("val"), spread, 0), 0)

    def component(field, index):
        tiles = field.reshape(2, 6, 8, 18, 128).transpose(0, 1, 3, 2, 4).reshape(2, 108, 8, 128)
        picked = lax.dynamic_index_in_dim(tiles, index, 0, False).astype(jnp.float16)
        return jnp.pad(picked, ((0, 4), (0, 0), (0, 0)))

    swap = [(i, i ^ 1) for i in range(n_col)]
    theirs = component(valence_store[0, 0], 1 - core)
    other = lax.ppermute(theirs, "col", swap)
    mine = lax.optimization_barrier(component(lax.optimization_barrier(valence_store)[0, 0], core))
    half = jnp.where((owner & 1)[None, None, :] == core, mine, other)
    source = lax.iota(jnp.int32, chips)[:, None] == (owner >> 1)[None, :]
    half, source = lax.optimization_barrier((half, source))
    groups = [[q * 2 + c for q in range(chips)] for c in range(2)]
    got = lax.all_to_all(half.reshape(chips, 7, 8, 128), "col", 0, 0, tiled=True, axis_index_groups=groups)
    got, gvec_index = lax.optimization_barrier((got, gvec_index))
    words, spots = gather_words(gvec_index)
    chunk = jnp.sum(jnp.where(source[:, None, None, :], got, 0).astype(F32), 0, keepdims=True)
    again = jnp.broadcast_to(chunk.astype(got.dtype), (chips, 7, 8, 128))
    again, words, spots = lax.optimization_barrier((again, words, spots))
    half = lax.all_to_all(again, "col", 0, 0, tiled=True, axis_index_groups=groups).reshape(112, 8, 128)
    half, cond_energy, valence_energy = lax.optimization_barrier((half, cond_energy, valence_energy))
    other = lax.ppermute(half, "col", swap)
    both = jnp.stack([jnp.where(core == 0, half, other), jnp.where(core == 0, other, half)], 0)
    valence = both[:, :108].reshape(2, 6, 18, 8, 128).transpose(0, 1, 3, 2, 4).reshape(2, L, L * L).astype(F32)

    total_bands = cond_bands.shape[0] * n_col * n_val
    constant = total_bands ** (-0.25) * L ** (-1.5)
    scaling = jnp.sqrt(2.0 / (cond_energy - valence_energy[0])) * constant
    scale = jnp.broadcast_to(scaling[:, None], (scaling.shape[0], 128))
    pairs = pair_elements(valence, cond_bands, scale, words, spots).reshape(n_col, 8, 128)

    row_count = ROW_DEV * n_val
    row_blocks = row_count // 128
    heads = pairs[:row_blocks]
    by_core = pairs.reshape(chips, 2, 8, 128)
    mine = lax.dynamic_index_in_dim(by_core, core, 1, False)
    theirs = lax.dynamic_index_in_dim(by_core, 1 - core, 1, False)
    other = lax.ppermute(jnp.concatenate([theirs, heads], 0), "col", swap)
    spread = lambda block: jnp.broadcast_to(block[None], (chips, row_blocks, 8, 128))
    sent = jnp.concatenate(
        [mine[:, None], spread(heads), other[:chips, None], spread(other[chips:])], 1
    )
    came = lax.all_to_all(sent, "col", 0, 0, tiled=True, axis_index_groups=groups)
    came = came.reshape(n_col, 1 + row_blocks, 8, 128)
    col = came[:, 0]
    turned = jnp.concatenate([-col[:, 4:], col[:, :4]], 1)
    right = jnp.concatenate([col, turned], 2).reshape(n_col * 8, 256)
    left = came[:, 1:].transpose(1, 0, 2, 3).reshape(row_blocks, n_col * 8, 128)
    part = -lax.dot_general(
        left, right, (((1,), (0,)), ((), ())), preferred_element_type=F32
    )
    part = part.reshape(n_val, ROW_DEV, 256).astype(BF)
    summands = lax.all_to_all(part, "val", 0, 0, tiled=True)
    total = jnp.sum(summands.astype(F32), 0)
    return total.reshape(ROW_DEV, 2, 128).transpose(1, 0, 2)


def solution(mesh):
    return jax.shard_map(
        local,
        mesh=mesh,
        in_specs=(
            P("val", "col", None, None, None),
            P(),
            P("val"),
            P("col", None, None, None),
            P("col"),
            P(),
        ),
        out_specs=P(None, "val", "col"),
        check_vma=False,
    )
```

```python
import numpy as np

import jax
import jax.numpy as jnp
from jax import lax
from jax.experimental import pallas as pl
from jax.experimental.pallas import tpu as pltpu
from jax.sharding import PartitionSpec as P

ROW_DEV = 64
L = 48
YI = 8
YB = L // YI
SLAB = YI * L
R1 = YB * L
K1 = 6 * L
K2 = 6 * SLAB
ROOT = 0.75 ** 0.5
BF = jnp.bfloat16
F32 = jnp.float32


def tables():
    def trig(phase):
        angle = 2.0 * np.pi * (phase % L) / L
        return np.stack([np.cos(angle), np.sin(angle)]).astype(np.float32)

    r = np.arange(L)
    ka_of = np.repeat(np.arange(YI), L)
    kz_of = np.tile(r, YI)
    t1 = trig(r[:, None] * r[None, :])
    t1 = np.block([[t1[0], t1[1]], [-t1[1], t1[0]]])
    t2a = trig(r[:, None] * kz_of[None, :])
    t2b = trig(6 * np.arange(YI)[:, None] * ka_of[None, :])
    yi_of = np.repeat(np.arange(YI), L)
    tw = trig(np.arange(8)[:, None] * yi_of[None, :])
    return t1, t2a, t2b, tw


def split(value):
    hi = value.astype(BF)
    return hi, (value - hi.astype(F32)).astype(BF)


def dft3(s):
    (r0, i0), (r1, i1), (r2, i2) = s
    tr, ti = r1 + r2, i1 + i2
    ur, ui = r0 - 0.5 * tr, i0 - 0.5 * ti
    dr, di = (r1 - r2) * ROOT, (i1 - i2) * ROOT
    return [(r0 + tr, i0 + ti), (ur + di, ui - dr), (ur - di, ui + dr)]


def dft6(p):
    a = [(p[m][0] + p[m + 3][0], p[m][1] + p[m + 3][1]) for m in range(3)]
    b = [(p[m][0] - p[m + 3][0], p[m][1] - p[m + 3][1]) for m in range(3)]
    b[1] = (p[4][0] - p[1][0], p[4][1] - p[1][1])
    even = dft3(a)
    odd = dft3(b)
    return [even[0], odd[2], even[1], odd[0], even[2], odd[1]]


def fill_tables(t1, t2a, t2b, a1, b2):
    hi, lo = split(t1[...])
    a1[:, 0:2 * L] = hi
    a1[:, 2 * L:4 * L] = lo
    a1[:, 4 * L:6 * L] = hi
    for yi in range(YI):
        cb = t2b[0, yi:yi + 1, :]
        sb = t2b[1, yi:yi + 1, :]
        cos = t2a[0] * cb - t2a[1] * sb
        sin = t2a[1] * cb + t2a[0] * sb
        for value, negative, spots in ((cos, False, ((0, 0), (1, 1))), (sin, True, ((1, 0), (0, 1)))):
            hi, lo = split(value)
            for ri, half in spots:
                flip = negative and ri == 0
                high, low = (-hi, -lo) if flip else (hi, lo)
                cols = slice(half * SLAB, (half + 1) * SLAB)
                r0 = ri * SLAB + yi * L
                b2[r0:r0 + L, cols] = high
                b2[2 * SLAB + r0:2 * SLAB + r0 + L, cols] = low
                b2[4 * SLAB + r0:4 * SLAB + r0 + L, cols] = high


def pairs_kernel(
    word_any, c_any, re_ref, im_ref, scale_ref, t1, t2a, t2b, tw, spot_ref, out_ref,
    word, c_ref, a1, b2, p3, l2, grid, hots, wide, sems, word_sem,
):
    def fetch(band):
        return pltpu.make_async_copy(c_any.at[band], c_ref.at[band], sems.at[band])

    word_copy = pltpu.make_async_copy(word_any, word, word_sem)
    for band in range(c_any.shape[0]):
        fetch(band).start()
    word_copy.start()
    fill_tables(t1, t2a, t2b, a1, b2)

    def bands(step, carry):
        for bb in range(2):
            fetch(2 * step + bb).wait()
            for lt in range(SLAB // 128):
                for xc in range(L // 16):
                    xs = slice(xc * 16, xc * 16 + 16)
                    cols = slice(bb * SLAB + lt * 128, bb * SLAB + lt * 128 + 128)
                    p = []
                    for yb in range(YB):
                        lanes = slice(yb * SLAB + lt * 128, yb * SLAB + lt * 128 + 128)
                        v0 = re_ref[xs, lanes]
                        v1 = im_ref[xs, lanes]
                        c0 = c_ref[2 * step + bb, 0, xs, lanes]
                        c1 = c_ref[2 * step + bb, 1, xs, lanes]
                        p.append((v0 * c0 + v1 * c1, v0 * c1 - v1 * c0))
                    for kb, q in enumerate(dft6(p)):
                        for ri in range(2):
                            hi, lo = split(q[ri])
                            r0 = ri * L + xc * 16
                            p3[kb, r0:r0 + 16, cols] = hi
                            p3[kb, 2 * L + r0:2 * L + r0 + 16, cols] = hi
                            p3[kb, 4 * L + r0:4 * L + r0 + 16, cols] = lo
        for kb in range(YB):
            z = jnp.dot(a1[...], p3[kb], preferred_element_type=F32)
            cw = tw[0, kb:kb + 1, :]
            sw = tw[1, kb:kb + 1, :]
            for bb in range(2):
                zr = z[:L, bb * SLAB:(bb + 1) * SLAB]
                zi = z[L:, bb * SLAB:(bb + 1) * SLAB]
                rows = slice(bb * R1 + kb * L, bb * R1 + kb * L + L)
                for ri, value in enumerate((zr * cw + zi * sw, zi * cw - zr * sw)):
                    hi, lo = split(value)
                    l2[rows, ri * SLAB:(ri + 1) * SLAB] = hi
                    l2[rows, (2 + ri) * SLAB:(3 + ri) * SLAB] = hi
                    l2[rows, (4 + ri) * SLAB:(5 + ri) * SLAB] = lo
        y = jnp.dot(l2[...], b2[...], preferred_element_type=F32)
        for bb in range(2):
            scale = scale_ref[pl.ds(2 * step + bb, 1), :]
            for ri in range(2):
                for t in range(3):
                    c0 = ri * SLAB + t * 128
                    start = t * 8 + ri * 4 + bb + 2 * step
                    grid[pl.ds(start, R1, stride=24), :] = y[bb * R1:(bb + 1) * R1, c0:c0 + 128] * scale
        return carry

    lax.fori_loop(0, 2, bands, 0)

    lane = lax.broadcasted_iota(jnp.int32, (128, 128), 1).astype(F32)
    own = lax.broadcasted_iota(jnp.int32, (8, 256), 1) % 8 == lax.broadcasted_iota(jnp.int32, (8, 256), 0)
    ones = jnp.ones((16, 128), BF)

    word_copy.wait()
    def one_hot(b):
        spots = jnp.broadcast_to(spot_ref[b:b + 1, :], (128, 128)).T
        hots[b % 2] = (spots == lane).astype(F32)

    one_hot(0)
    for b in range(spot_ref.shape[0]):
        hot = hots.at[b % 2]
        for j in range(4):
            if j == 1 and b + 1 < spot_ref.shape[0]:
                one_hot(b + 1)
            rows = []
            for i in range(32 * j, 32 * j + 32):
                start = pl.multiple_of(word[b * 128 + i], 8)
                rows.append(grid[pl.ds(start, 8), :] * jnp.broadcast_to(hot[i:i + 1, :], (8, 128)))
            sums = lax.dot_general(
                ones, jnp.concatenate(rows, 0).astype(BF),
                (((1,), (1,)), ((), ())), preferred_element_type=F32,
            )
            wide[b * 8:b * 8 + 8, j * 256:j * 256 + 256] = jnp.where(own, sums[:8], 0.0)
    fold = (
        lax.broadcasted_iota(jnp.int32, (1024, 128), 0) // 8
        == lax.broadcasted_iota(jnp.int32, (1024, 128), 1)
    ).astype(F32).astype(BF)
    out_ref[...] = jnp.dot(wide[...].astype(BF), fold, preferred_element_type=F32).astype(BF)


def pair_elements(valence, cond, scale, words, spots):
    count = words.shape[0]
    rows = count // 128 * 8
    vmem = pl.BlockSpec(memory_space=pltpu.VMEM)
    hbm = pl.BlockSpec(memory_space=pltpu.HBM)
    cond = pltpu.with_memory_space_constraint(cond, pltpu.HBM)
    return pl.pallas_call(
        pairs_kernel,
        out_shape=jax.ShapeDtypeStruct((rows, 128), BF),
        in_specs=[hbm, hbm] + [vmem] * 8,
        out_specs=vmem,
        scratch_shapes=[
            pltpu.SMEM((count,), jnp.int32),
            pltpu.VMEM(cond.shape, F32),
            pltpu.VMEM((2 * L, K1), BF),
            pltpu.VMEM((K2, 2 * SLAB), BF),
            pltpu.VMEM((YB, K1, 2 * SLAB), BF),
            pltpu.VMEM((2 * R1, K2), BF),
            pltpu.VMEM((R1 * 24, 128), F32),
            pltpu.VMEM((2, 128, 128), F32),
            pltpu.VMEM((rows, 1024), F32),
            pltpu.SemaphoreType.DMA((cond.shape[0],)),
            pltpu.SemaphoreType.DMA(()),
        ],
        compiler_params=pltpu.CompilerParams(vmem_limit_bytes=40 << 20),
        name="pairs",
    )(words, cond, *valence, scale, *tables(), spots)


def gather_words(gvec_index):
    kx = gvec_index // (L * L)
    ky = gvec_index // L % L
    kz = gvec_index % L
    lane = ky // YB * L + kz
    tile = (ky % YB * L + kx) * 3 + lane // 128
    return tile * 8, (lane % 128).astype(F32).reshape(-1, 128)


def local(valence_store, band_owner, valence_energy, cond_bands, cond_energy, gvec_index):
    n_col = lax.axis_size("col")
    n_val = lax.axis_size("val")
    chips = n_col // 2
    core = lax.axis_index("col") & 1
    bands = lax.iota(jnp.int32, band_owner.shape[0])
    spread = jnp.broadcast_to(band_owner[:, None], (band_owner.shape[0], 128))
    owner = jnp.sum(jnp.where(bands[:, None] == lax.axis_index("val"), spread, 0), 0)

    def component(field, index):
        tiles = field.reshape(2, 6, 8, 18, 128).transpose(0, 1, 3, 2, 4).reshape(2, 108, 8, 128)
        picked = lax.dynamic_index_in_dim(tiles, index, 0, False).astype(jnp.float16)
        return jnp.pad(picked, ((0, 4), (0, 0), (0, 0)))

    swap = [(i, i ^ 1) for i in range(n_col)]
    theirs = component(valence_store[0, 0], 1 - core)
    other = lax.ppermute(theirs, "col", swap)
    mine = lax.optimization_barrier(component(lax.optimization_barrier(valence_store)[0, 0], core))
    half = jnp.where((owner & 1)[None, None, :] == core, mine, other)
    source = lax.iota(jnp.int32, chips)[:, None] == (owner >> 1)[None, :]
    half, source = lax.optimization_barrier((half, source))
    groups = [[q * 2 + c for q in range(chips)] for c in range(2)]
    got = lax.all_to_all(half.reshape(chips, 7, 8, 128), "col", 0, 0, tiled=True, axis_index_groups=groups)
    got, gvec_index = lax.optimization_barrier((got, gvec_index))
    words, spots = gather_words(gvec_index)
    chunk = jnp.sum(jnp.where(source[:, None, None, :], got, 0).astype(F32), 0, keepdims=True)
    again = jnp.broadcast_to(chunk.astype(got.dtype), (chips, 7, 8, 128))
    again, words, spots = lax.optimization_barrier((again, words, spots))
    half = lax.all_to_all(again, "col", 0, 0, tiled=True, axis_index_groups=groups).reshape(112, 8, 128)
    half, cond_energy, valence_energy = lax.optimization_barrier((half, cond_energy, valence_energy))
    other = lax.ppermute(half, "col", swap)
    def plain(block):
        return block[:108].reshape(6, 18, 8, 128).transpose(0, 2, 1, 3).reshape(L, L * L).astype(F32)

    valence = plain(jnp.where(core == 0, half, other)), plain(jnp.where(core == 0, other, half))

    total_bands = cond_bands.shape[0] * n_col * n_val
    constant = total_bands ** (-0.25) * L ** (-1.5)
    scaling = jnp.sqrt(2.0 / (cond_energy - valence_energy[0])) * constant
    scale = jnp.broadcast_to(scaling[:, None], (scaling.shape[0], 128))
    pairs = pair_elements(valence, cond_bands, scale, words, spots).reshape(n_col, 8, 128)

    row_count = ROW_DEV * n_val
    row_blocks = row_count // 128
    heads = pairs[:row_blocks]
    by_core = pairs.reshape(chips, 2, 8, 128)
    mine = lax.dynamic_index_in_dim(by_core, core, 1, False)
    theirs = lax.dynamic_index_in_dim(by_core, 1 - core, 1, False)
    other = lax.ppermute(jnp.concatenate([theirs, heads], 0), "col", swap)
    spread = lambda block: jnp.broadcast_to(block[None], (chips, row_blocks, 8, 128))
    sent = jnp.concatenate(
        [mine[:, None], spread(heads), other[:chips, None], spread(other[chips:])], 1
    )
    came = lax.all_to_all(sent, "col", 0, 0, tiled=True, axis_index_groups=groups)
    came = came.reshape(n_col, 1 + row_blocks, 8, 128)
    col = came[:, 0]
    turned = jnp.concatenate([-col[:, 4:], col[:, :4]], 1)
    right = jnp.concatenate([col, turned], 2).reshape(n_col * 8, 256)
    left = came[:, 1:].transpose(1, 0, 2, 3).reshape(row_blocks, n_col * 8, 128)
    part = -lax.dot_general(
        left, right, (((1,), (0,)), ((), ())), preferred_element_type=F32
    )
    part = part.reshape(n_val, ROW_DEV, 256).astype(BF)
    summands = lax.all_to_all(part, "val", 0, 0, tiled=True)
    total = jnp.sum(summands.astype(F32), 0)
    return jnp.stack([total[:, :128], total[:, 128:]], 0)


def solution(mesh):
    return jax.shard_map(
        local,
        mesh=mesh,
        in_specs=(
            P("val", "col", None, None, None),
            P(),
            P("val"),
            P("col", None, None, None),
            P("col"),
            P(),
        ),
        out_specs=P(None, "val", "col"),
        check_vma=False,
    )
```
